256 devices in a mesh: gx: 8 (over x, core), gy: 4 (over y), gz: 8 (over z).
Axes of the slice: x: 4, y: 4, z: 8, core: 2. Of those that a mesh axis runs over, the one named last changes fastest.
Arguments:
- segments: float32 [16384, 12, 128], P(('gx', 'gy', 'gz')), may hold values from -8 to 8, as said below
- remesh_matrix: float32 [128, 128], replicated, may hold values from -1 to 2, as said below
- ghost_list: int32 [256, 8, 4], P(('gx', 'gy', 'gz')), may hold values from 0 to 63
- pair_list: int32 [256, 512, 2], P(('gx', 'gy', 'gz')), may hold values from 0 to 159, as said below
- tile_count: int32 [256], P(('gx', 'gy', 'gz')), may hold values from 128 to 512, as said below
- cut_axis: int32 [3], replicated, may hold values from 0 to 2, each once
- mig_list: int32 [256, 3, 24], P(('gx', 'gy', 'gz')), may hold values from 0 to 63, as said below
- mig_count: int32 [256, 3], P(('gx', 'gy', 'gz')), may hold values from 8 to 24
Outputs:
- segments_out: float32 [16384, 12, 128], P(('gx', 'gy', 'gz'))
The draws below stay inside these ranges and needn't reach their ends.
Inputs may be any that keep to these rules, and one draw needn't show every extreme that they name: `segments`: components 0-2 and 3-5 are real values, 6-8 smaller ones, and 9-11 lie between 0.3 and 3. `remesh_matrix`: A dominant diagonal near 0.7 with dense independent entries beside it. `pair_list`: the first entry of a row is one of the domain's own blocks, below 64; the second indexes the domain's own blocks followed by its 96 ghost blocks. `tile_count`: in every draw some domain uses all 512 rows. `cut_axis`: each of the three directions is cut at exactly one step. `mig_list`: the entries of one domain's list for one step differ from each other.
All inputs are finite; a program needn't handle non-finite values.
Results may differ from the reference program's by a relative error of at most 0.00055.
Values sent between devices are 32-bit elements; how exact they have to be, the bound alone decides.
A program may use at most 64 MiB of HBM per device.

```python
import jax
import jax.numpy as jnp
from jax import lax

SB = 128
NB = 64
GQ = 4
P_SIZE = 512
MIG_MAX = 24
MIG_MIN = 8
STEPS = 3
DOMAINS = 256
BLOCKS = 16384
N_GX = 8
N_GY = 4
N_GZ = 8


def draw_segments(key, part):
    keys = jax.random.split(key, 4)
    places = jnp.clip(jax.random.normal(keys[0], (BLOCKS, 3, SB), jnp.float32), -4.0, 4.0)
    burgers = jnp.clip(jax.random.normal(keys[1], (BLOCKS, 3, SB), jnp.float32), -4.0, 4.0)
    previous = jnp.clip(0.5 * jax.random.normal(keys[2], (BLOCKS, 3, SB), jnp.float32), -2.0, 2.0)
    mobility = jnp.exp(jax.random.uniform(keys[3], (BLOCKS, 3, SB), jnp.float32, jnp.log(0.3), jnp.log(3.0)))
    return jnp.concatenate([places, burgers, previous, mobility], axis=1)


def draw_remesh_matrix(key, part):
    noise = jnp.clip(jax.random.normal(key, (SB, SB), jnp.float32), -4.0, 4.0)
    return 0.7 * jnp.eye(SB, dtype=jnp.float32) + 0.3 * noise / jnp.sqrt(SB * 1.0)


def draw_pair_list(key, part):
    keys = jax.random.split(jax.random.fold_in(key, 11), 2)
    targets = jax.random.randint(keys[0], (DOMAINS, P_SIZE, 1), 0, NB, dtype=jnp.int32)
    sources_idx = jax.random.randint(keys[1], (DOMAINS, P_SIZE, 1), 0, NB + 24 * GQ, dtype=jnp.int32)
    return jnp.concatenate([targets, sources_idx], axis=2)


def draw_tile_count(key, part):
    keys = jax.random.split(jax.random.fold_in(key, 23), 2)
    counts = jax.random.randint(keys[0], (DOMAINS,), P_SIZE // 4, P_SIZE + 1, dtype=jnp.int32)
    busiest = jax.random.randint(keys[1], (), 0, DOMAINS, dtype=jnp.int32)
    return counts.at[busiest].set(P_SIZE)


def draw_mig_list(key, part):
    keys = jax.random.split(jax.random.fold_in(key, 37), DOMAINS * STEPS)
    chosen = jax.vmap(lambda single: jax.random.permutation(single, NB)[:MIG_MAX])(keys)
    return chosen.reshape(DOMAINS, STEPS, MIG_MAX).astype(jnp.int32)


def touch_ends(result, stream_key, low, high):
    longest = result.shape.index(max(result.shape))
    spots = []
    for shift in (0, 1):
        where = [jax.random.randint(jax.random.fold_in(stream_key, axis), (), 0, length) for axis, length in enumerate(result.shape)]
        where[longest] = (where[longest] + shift) % result.shape[longest]
        spots.append(tuple(where))
    return result.at[spots[0]].set(low).at[spots[1]].set(high)


def setup_inputs(seed: int = 0) -> dict:
    splits = jax.random.split(jax.random.key(seed), 9)
    segments = draw_segments(jax.random.fold_in(splits[8], 71), 0)
    remesh_matrix = draw_remesh_matrix(jax.random.fold_in(splits[8], 71), 0)
    ghost_list = touch_ends(jax.random.randint(splits[2], (DOMAINS, 8, GQ), 0, NB), jax.random.fold_in(splits[2], 1), 0, NB - 1).astype(jnp.int32)
    pair_list = draw_pair_list(jax.random.fold_in(splits[8], 71), 0)
    tile_count = draw_tile_count(jax.random.fold_in(splits[8], 71), 0)
    cut_axis = jax.random.permutation(splits[5], 3).astype(jnp.int32)
    mig_list = draw_mig_list(jax.random.fold_in(splits[8], 71), 0)
    mig_count = touch_ends(jax.random.randint(splits[7], (DOMAINS, STEPS), MIG_MIN, MIG_MAX + 1), jax.random.fold_in(splits[7], 1), MIG_MIN, MIG_MAX).astype(jnp.int32)
    return dict(segments=segments, remesh_matrix=remesh_matrix, ghost_list=ghost_list, pair_list=pair_list, tile_count=tile_count, cut_axis=cut_axis, mig_list=mig_list, mig_count=mig_count)


core_square = 0.1
time_step = 0.5
stress_coef = 0.25


def source_terms(blocks):
    burgers = blocks[..., 3:6, :]
    return jnp.stack([burgers[..., 0, :] * burgers[..., 0, :], burgers[..., 1, :] * burgers[..., 1, :],
                      burgers[..., 2, :] * burgers[..., 2, :], burgers[..., 0, :] * burgers[..., 1, :],
                      burgers[..., 1, :] * burgers[..., 2, :], burgers[..., 0, :] * burgers[..., 2, :]],
                     axis=-2).astype(jnp.bfloat16)


def tile_weights(target_places, source_places):
    offsets_xyz = target_places[:, :, :, None] - source_places[:, :, None, :]
    squared = jnp.sum(offsets_xyz * offsets_xyz, axis=1)
    return (1.0 / (squared + core_square)).astype(jnp.bfloat16)


def domain_stress(combined, pairs, count_now):
    places = combined[:, 0:3]
    terms = source_terms(combined)
    targets = pairs[:, 0]
    sources_idx = pairs[:, 1]
    weights = tile_weights(places[targets], places[sources_idx])
    contrib = jnp.einsum("kmb,kab->kma", terms[sources_idx].astype(jnp.float32), weights.astype(jnp.float32))
    valid = jnp.arange(pairs.shape[0]) < count_now
    contrib = jnp.where(valid[:, None, None], contrib, 0.0)
    return jax.ops.segment_sum(contrib, targets, num_segments=NB) * (stress_coef / SB)


def advance(state, stress_field):
    places = state[..., 0:3, :]
    burgers = state[..., 3:6, :]
    previous = state[..., 6:9, :]
    mobility = state[..., 9:12, :]
    sxx, syy, szz = stress_field[..., 0, :], stress_field[..., 1, :], stress_field[..., 2, :]
    sxy, syz, sxz = stress_field[..., 3, :], stress_field[..., 4, :], stress_field[..., 5, :]
    force_x = sxx * burgers[..., 0, :] + sxy * burgers[..., 1, :] + sxz * burgers[..., 2, :]
    force_y = sxy * burgers[..., 0, :] + syy * burgers[..., 1, :] + syz * burgers[..., 2, :]
    force_z = sxz * burgers[..., 0, :] + syz * burgers[..., 1, :] + szz * burgers[..., 2, :]
    velocity = mobility * jnp.stack([force_x, force_y, force_z], axis=-2)
    places = places + time_step * (1.5 * velocity - 0.5 * previous)
    return jnp.concatenate([places, burgers, velocity, mobility], axis=-2)


def remesh(state, remesh_matrix):
    places = jnp.einsum("...ca,ab->...cb", state[..., 0:3, :], remesh_matrix, precision=lax.Precision.HIGHEST)
    return jnp.concatenate([places, state[..., 3:, :]], axis=-2)


def ghost_faces(octants):
    grid = octants.reshape(N_GX, N_GY, N_GZ, 2, 2, 2, GQ, 6, SB)
    face_list = [jnp.roll(grid, 1, 0)[:, :, :, 1], jnp.roll(grid, -1, 0)[:, :, :, 0],
                 jnp.roll(grid, 1, 1)[:, :, :, :, 1], jnp.roll(grid, -1, 1)[:, :, :, :, 0],
                 jnp.roll(grid, 1, 2)[:, :, :, :, :, 1], jnp.roll(grid, -1, 2)[:, :, :, :, :, 0]]
    return jnp.concatenate([face.reshape(DOMAINS, 4 * GQ, 6, SB) for face in face_list], axis=1)


def reference(segments, remesh_matrix, ghost_list, pair_list, tile_count, cut_axis, mig_list, mig_count):
    state = segments.reshape(DOMAINS, NB, 12, SB)
    domain_ids = jnp.arange(DOMAINS, dtype=jnp.int32)
    partner_bits = jnp.array([(N_GX // 2) * N_GY * N_GZ, (N_GY // 2) * N_GZ, N_GZ // 2], dtype=jnp.int32)
    for step_index in range(STEPS):
        sources_now = state[:, :, 0:6]
        octants = jax.vmap(lambda blocks_now, lists_now: blocks_now[lists_now])(sources_now, ghost_list)
        combined = jnp.concatenate([sources_now, ghost_faces(octants)], axis=1)
        stress_field = lax.map(lambda items: domain_stress(items[0], items[1], items[2]),
                               (combined, pair_list, tile_count))
        state = remesh(advance(state, stress_field), remesh_matrix)
        partner = jnp.bitwise_xor(domain_ids, partner_bits[cut_axis[step_index]])
        keep_count = jnp.minimum(mig_count[:, step_index], mig_count[partner, step_index])
        slot_lists = mig_list[:, step_index]
        incoming = state[partner[:, None], slot_lists[partner]]
        current = state[domain_ids[:, None], slot_lists]
        live_slots = jnp.arange(MIG_MAX)[None, :] < keep_count[:, None]
        state = state.at[domain_ids[:, None], slot_lists].set(jnp.where(live_slots[:, :, None, None], incoming, current))
    return state.reshape(BLOCKS, 12, SB)
```

```python
import functools

import jax
import jax.numpy as jnp
from jax import lax
from jax.experimental import pallas as pl
from jax.experimental.pallas import tpu as pltpu
from jax.sharding import PartitionSpec as P

STEPS = 3
MESH = pl.DeviceIdType.MESH

core_square = 0.1
time_step = 0.5
stress_coef = 0.25

GROUP = 16


def layout_of(tiles, blocks, ghosts, slots):
    sizes = dict(
        target=tiles,
        source=tiles,
        term=tiles,
        keep=tiles,
        last=blocks,
        ghost=ghosts,
        mig=STEPS * slots,
        rank=STEPS * blocks,
        cut=STEPS,
        count=STEPS,
    )
    offsets, total = {}, 0
    for name, size in sizes.items():
        offsets[name] = total
        total += size
    return offsets, total


def index_table(ghost_list, pair_list, tile_count, cut_axis, mig_list, mig_count, blocks, sources):
    tiles = pair_list.shape[1]
    targets, origin = pair_list[0, :, 0], pair_list[0, :, 1]
    number = jnp.arange(tiles, dtype=jnp.int32)
    dead = (number >= tile_count[0]).astype(jnp.int32)
    key = targets * tiles + number
    place = jnp.sum((key[None, :] < key[:, None]).astype(jnp.int32), axis=1)
    packed = (targets * 1024 + origin) * 2 + dead
    hit = place[None, :] == number[:, None]
    ordered = jnp.sum(jnp.where(hit, packed[None, :], 0), axis=1)
    target = ordered // 2048
    source = (ordered // 2) % 1024
    term = jnp.where(ordered % 2 == 1, sources, source)
    before = jnp.concatenate([jnp.full((1,), -1, jnp.int32), target[:-1]])
    keep = (target == before).astype(jnp.int32)
    slot = jnp.arange(blocks, dtype=jnp.int32)
    upto = jnp.sum((targets[None, :] <= slot[:, None]).astype(jnp.int32), axis=1)
    own = jnp.sum((targets[None, :] == slot[:, None]).astype(jnp.int32), axis=1)
    last = jnp.where(own > 0, upto - 1, tiles)
    lists = mig_list[0]
    capacity = lists.shape[1]
    match = lists[:, None, :] == slot[None, :, None]
    order = jnp.arange(capacity, dtype=jnp.int32)
    rank = jnp.min(jnp.where(match, order[None, None, :], capacity), axis=2)
    return jnp.concatenate(
        [
            target,
            source,
            term,
            keep,
            last,
            ghost_list[0].reshape(-1),
            lists.reshape(-1),
            rank.reshape(-1),
            cut_axis,
            mig_count[0],
        ]
    )


def kernel(
    at,
    sizes,
    table,
    segments,
    matrix,
    result,
    geo,
    inv,
    own,
    src,
    terms,
    spread,
    sums,
    field,
    got,
    ghost_out,
    ghost_in,
    inv_out,
    inv_in,
    geo_out,
    geo_in,
    ghost_send,
    ghost_recv,
    inv_send,
    inv_recv,
    geo_send,
    geo_recv,
):
    blocks, tiles, ghosts, capacity = sizes
    width = segments.shape[2]
    here = tuple(lax.axis_index(name) for name in ("gx", "gy", "gz"))

    def shifted(axis, by):
        count = lax.axis_size(("gx", "gy", "gz")[axis])
        place = list(here)
        place[axis] = lax.rem(here[axis] + (by % count), count)
        return tuple(place)

    neighbours = []
    for axis in range(3):
        neighbours += [shifted(axis, 1), shifted(axis, -1)]
    partners = [
        shifted(axis, lax.axis_size(name) // 2) for axis, name in enumerate(("gx", "gy", "gz"))
    ]

    barrier = pltpu.get_barrier_semaphore()
    for device in neighbours + partners:
        pl.semaphore_signal(barrier, inc=1, device_id=device, device_id_type=MESH)

    row = lax.broadcasted_iota(jnp.int32, (8, width), 0)

    def rows(ref, i, count=8):
        return ref[pl.ds(i, count, stride=blocks), :]

    def load_state(i, carry):
        block = segments[i]
        geo[pl.ds(i, 3, stride=blocks), :] = block[0:3]
        geo[pl.ds(3 * blocks + i, 3, stride=blocks), :] = block[6:9]
        inv[pl.ds(i, 3, stride=blocks), :] = block[9:12]
        inv[pl.ds(3 * blocks + i, 3, stride=blocks), :] = block[3:6]
        return carry

    geo[6 * blocks : 8 * blocks, :] = jnp.zeros((2 * blocks, width), jnp.float32)
    inv[6 * blocks : 8 * blocks, :] = jnp.zeros((2 * blocks, width), jnp.float32)
    lax.fori_loop(0, blocks, load_state, 0, unroll=8)
    terms[blocks + ghosts] = jnp.zeros((8, width), jnp.float32)
    sums[tiles] = jnp.zeros((8, width), jnp.float32)
    pl.semaphore_wait(barrier, 9)

    def products(block):
        first = jnp.where(
            row >= 6, pltpu.roll(block, 3, 0), jnp.where(row == 2, pltpu.roll(block, 7, 0), block)
        )
        second = jnp.where(
            row >= 6, pltpu.roll(block, 2, 0), jnp.where(row == 2, pltpu.roll(block, 5, 0), block)
        )
        second = jnp.where(
            (row >= 3) & (row < 6), block, second
        )
        return first * second

    def ghost_copy(s, face):
        axis, low = face // 2, face % 2
        octants = ghost_out.at[s]
        bit = 1 - low
        part = (octants.at[bit], octants.at[:, bit], octants.at[:, :, bit])[axis]
        return pltpu.make_async_remote_copy(
            src_ref=part,
            dst_ref=ghost_in.at[s, face],
            send_sem=ghost_send.at[s, face],
            recv_sem=ghost_recv.at[s, face],
            device_id=neighbours[face],
            device_id_type=MESH,
        )

    def partner_copy(source, landing, send, recv, s, axis):
        return pltpu.make_async_remote_copy(
            src_ref=source.at[s],
            dst_ref=landing.at[s, axis],
            send_sem=send.at[s, axis],
            recv_sem=recv.at[s, axis],
            device_id=partners[axis],
            device_id_type=MESH,
        )

    def step(s, carry):
        def own_block(i, c):
            block = jnp.where(row < 3, rows(geo, i), rows(inv, i))
            own[i] = block
            src[i] = block
            terms[i] = products(block)
            return c

        lax.fori_loop(0, blocks, own_block, 0, unroll=8)

        for o in range(8):
            for q in range(4):
                pick = table[at["ghost"] + o * 4 + q]
                ghost_out[s, o // 4, (o // 2) % 2, o % 2, q] = own[pick]
        for face in range(6):
            ghost_copy(s, face).start()

        my_count = table[at["count"] + s].astype(jnp.float32)

        def out_inv(r, c):
            slot = table[at["mig"] + s * capacity + r]
            inv_out[s, r] = rows(inv, slot)
            return c

        lax.fori_loop(0, capacity, out_inv, 0, unroll=8)
        inv_out[s, capacity] = jnp.full((8, width), my_count, jnp.float32)
        for axis in range(3):
            partner_copy(inv_out, inv_in, inv_send, inv_recv, s, axis).start()

        def spread_block(i, c):
            turned = own[i].T
            for k in range(3):
                spread[i, k] = jnp.broadcast_to(turned[:, k : k + 1], (width, width))
            return c

        lax.fori_loop(0, blocks, spread_block, 0, unroll=4)

        for face in range(6):
            ghost_copy(s, face).wait_recv()

            def ghost_block(q, c, face=face):
                for u in range(4):
                    block = ghost_in[s, face, q // 2, q % 2, u]
                    spot = blocks + face * 16 + q * 4 + u
                    src[spot] = block
                    terms[spot] = products(block)
                return c

            lax.fori_loop(0, 4, ghost_block, 0, unroll=2)

        def tile_group(g, run):
            for u in range(0, GROUP, 2):
                weights, factors = [], []
                for v in range(2):
                    t = g * GROUP + u + v
                    i, j = table[at["target"] + t], table[at["source"] + t]
                    squared = None
                    for k in range(3):
                        offset = spread[i, k] - src[j, pl.ds(k, 1), :]
                        offset = offset * offset
                        squared = offset if squared is None else squared + offset
                    weights.append((1.0 / (squared + core_square)).astype(jnp.bfloat16))
                    factors.append(terms[table[at["term"] + t]])
                both = lax.dot_general(
                    jnp.concatenate(factors, axis=0).astype(jnp.bfloat16),
                    jnp.concatenate(weights, axis=0),
                    (((1,), (1,)), ((), ())),
                    preferred_element_type=jnp.float32,
                )
                for v in range(2):
                    t = g * GROUP + u + v
                    part = both[8 * v : 8 * v + 8, v * width : (v + 1) * width]
                    run = jnp.where(table[at["keep"] + t] != 0, run, 0.0) + part
                    sums[t] = run
            return run

        lax.fori_loop(0, tiles // GROUP, tile_group, jnp.zeros((8, width), jnp.float32))

        def collect(i, c):
            field[pl.ds(i, 8, stride=blocks), :] = sums[table[at["last"] + i]]
            return c

        lax.fori_loop(0, blocks, collect, 0, unroll=8)

        def comp(ref, k):
            return ref[k * blocks : (k + 1) * blocks, :]

        scale = stress_coef / width
        sxx, syy, szz = (comp(field, k) * scale for k in (3, 4, 5))
        sxy, syz, sxz = (comp(field, k) * scale for k in (6, 7, 2))
        b = [comp(inv, k) for k in (3, 4, 5)]
        force = (
            sxx * b[0] + sxy * b[1] + sxz * b[2],
            sxy * b[0] + syy * b[1] + syz * b[2],
            sxz * b[0] + syz * b[1] + szz * b[2],
        )
        for k in range(3):
            velocity = comp(inv, k) * force[k]
            previous = comp(geo, 3 + k)
            geo[k * blocks : (k + 1) * blocks, :] = comp(geo, k) + time_step * (
                1.5 * velocity - 0.5 * previous
            )
            geo[(3 + k) * blocks : (4 + k) * blocks, :] = velocity
        geo[0 : 3 * blocks, :] = jnp.dot(
            geo[0 : 3 * blocks, :],
            matrix[...],
            precision=lax.Precision.HIGHEST,
            preferred_element_type=jnp.float32,
        )

        def out_geo(r, c):
            slot = table[at["mig"] + s * capacity + r]
            geo_out[s, r] = rows(geo, slot)
            return c

        lax.fori_loop(0, capacity, out_geo, 0, unroll=8)
        for axis in range(3):
            partner_copy(geo_out, geo_in, geo_send, geo_recv, s, axis).start()
        for axis in range(3):
            partner_copy(inv_out, inv_in, inv_send, inv_recv, s, axis).wait_recv()
        cut = table[at["cut"] + s]

        def chosen(landing, r):
            later = jnp.where(cut == 1, landing[s, 1, r], landing[s, 2, r])
            return jnp.where(cut == 0, landing[s, 0, r], later)

        limit = jnp.minimum(chosen(inv_in, capacity), my_count)

        def take(ref, landing):
            def gather(r, c):
                got[r] = chosen(landing, r)
                return c

            lax.fori_loop(0, capacity, gather, 0, unroll=8)

            def body(i, c):
                r = table[at["rank"] + s * blocks + i]
                arrived = got[jnp.minimum(r, capacity - 1)]
                live = limit > r.astype(jnp.float32)
                ref[pl.ds(i, 8, stride=blocks), :] = jnp.where(live, arrived, rows(ref, i))
                return c

            lax.fori_loop(0, blocks, body, 0, unroll=8)

        take(inv, inv_in)
        for axis in range(3):
            partner_copy(geo_out, geo_in, geo_send, geo_recv, s, axis).wait_recv()
        take(geo, geo_in)
        for face in range(6):
            ghost_copy(s, face).wait_send()
        for axis in range(3):
            partner_copy(inv_out, inv_in, inv_send, inv_recv, s, axis).wait_send()
            partner_copy(geo_out, geo_in, geo_send, geo_recv, s, axis).wait_send()
        return carry

    lax.fori_loop(0, STEPS, step, 0)

    def store_state(i, carry):
        g, v = rows(geo, i), rows(inv, i)
        result[i, 0:3, :] = g[0:3]
        result[i, 3:6, :] = v[3:6]
        result[i, 6:9, :] = g[3:6]
        result[i, 9:12, :] = v[0:3]
        return carry

    lax.fori_loop(0, blocks, store_state, 0, unroll=8)


def on_device(
    segments, remesh_matrix, ghost_list, pair_list, tile_count, cut_axis, mig_list, mig_count
):
    blocks, _, width = segments.shape
    tiles = pair_list.shape[1]
    per_cell = ghost_list.shape[2]
    ghosts = 24 * per_cell
    capacity = mig_list.shape[2]
    at, _ = layout_of(tiles, blocks, 8 * per_cell, capacity)
    table = index_table(
        ghost_list, pair_list, tile_count, cut_axis, mig_list, mig_count, blocks, blocks + ghosts
    )
    vmem = pl.BlockSpec(memory_space=pltpu.VMEM)
    f32 = jnp.float32
    return pl.pallas_call(
        functools.partial(kernel, at, (blocks, tiles, ghosts, capacity)),
        out_shape=jax.ShapeDtypeStruct(segments.shape, f32),
        in_specs=[pl.BlockSpec(memory_space=pltpu.SMEM), vmem, vmem],
        out_specs=vmem,
        scratch_shapes=[
            pltpu.VMEM((8 * blocks, width), f32),
            pltpu.VMEM((8 * blocks, width), f32),
            pltpu.VMEM((blocks, 8, width), f32),
            pltpu.VMEM((blocks + ghosts, 8, width), f32),
            pltpu.VMEM((blocks + ghosts + 1, 8, width), f32),
            pltpu.VMEM((blocks, 3, width, width), f32),
            pltpu.VMEM((tiles + 1, 8, width), f32),
            pltpu.VMEM((8 * blocks, width), f32),
            pltpu.VMEM((capacity, 8, width), f32),
            pltpu.VMEM((STEPS, 2, 2, 2, per_cell, 8, width), f32),
            pltpu.VMEM((STEPS, 6, 2, 2, per_cell, 8, width), f32),
            pltpu.VMEM((STEPS, capacity + 1, 8, width), f32),
            pltpu.VMEM((STEPS, 3, capacity + 1, 8, width), f32),
            pltpu.VMEM((STEPS, capacity, 8, width), f32),
            pltpu.VMEM((STEPS, 3, capacity, 8, width), f32),
            pltpu.SemaphoreType.DMA((STEPS, 6)),
            pltpu.SemaphoreType.DMA((STEPS, 6)),
            pltpu.SemaphoreType.DMA((STEPS, 3)),
            pltpu.SemaphoreType.DMA((STEPS, 3)),
            pltpu.SemaphoreType.DMA((STEPS, 3)),
            pltpu.SemaphoreType.DMA((STEPS, 3)),
        ],
        compiler_params=pltpu.CompilerParams(
            collective_id=0, has_side_effects=True, vmem_limit_bytes=48 * 1024 * 1024
        ),
    )(table, segments, remesh_matrix)


def solution(mesh):
    return jax.shard_map(
        on_device,
        mesh=mesh,
        in_specs=(
            P(("gx", "gy", "gz"), None, None),
            P(),
            P(("gx", "gy", "gz"), None, None),
            P(("gx", "gy", "gz"), None, None),
            P(("gx", "gy", "gz")),
            P(),
            P(("gx", "gy", "gz"), None, None),
            P(("gx", "gy", "gz"), None),
        ),
        out_specs=P(("gx", "gy", "gz"), None, None),
        check_vma=False,
    )
```

```python
import functools

import jax
import jax.numpy as jnp
from jax import lax
from jax.experimental import pallas as pl
from jax.experimental.pallas import tpu as pltpu
from jax.sharding import PartitionSpec as P

STEPS = 3
MESH = pl.DeviceIdType.MESH

core_square = 0.1
time_step = 0.5
stress_coef = 0.25

GROUP = 16


def layout_of(tiles, blocks, ghosts, slots):
    sizes = dict(
        target=tiles,
        source=tiles,
        term=tiles,
        keep=tiles,
        last=blocks,
        ghost=ghosts,
        mig=STEPS * slots,
        rank=STEPS * blocks,
        cut=STEPS,
        count=STEPS,
    )
    offsets, total = {}, 0
    for name, size in sizes.items():
        offsets[name] = total
        total += size
    return offsets, total


def index_table(ghost_list, pair_list, tile_count, cut_axis, mig_list, mig_count, blocks, sources):
    tiles = pair_list.shape[1]
    targets, origin = pair_list[0, :, 0], pair_list[0, :, 1]
    number = jnp.arange(tiles, dtype=jnp.int32)
    dead = (number >= tile_count[0]).astype(jnp.int32)
    key = targets * tiles + number
    place = jnp.sum((key[None, :] < key[:, None]).astype(jnp.int32), axis=1)
    packed = (targets * 1024 + origin) * 2 + dead
    hit = place[None, :] == number[:, None]
    ordered = jnp.sum(jnp.where(hit, packed[None, :], 0), axis=1)
    target = ordered // 2048
    source = (ordered // 2) % 1024
    term = jnp.where(ordered % 2 == 1, sources, source)
    before = jnp.concatenate([jnp.full((1,), -1, jnp.int32), target[:-1]])
    keep = (target == before).astype(jnp.int32)
    slot = jnp.arange(blocks, dtype=jnp.int32)
    upto = jnp.sum((targets[None, :] <= slot[:, None]).astype(jnp.int32), axis=1)
    own = jnp.sum((targets[None, :] == slot[:, None]).astype(jnp.int32), axis=1)
    last = jnp.where(own > 0, upto - 1, tiles)
    lists = mig_list[0]
    capacity = lists.shape[1]
    match = lists[:, None, :] == slot[None, :, None]
    order = jnp.arange(capacity, dtype=jnp.int32)
    rank = jnp.min(jnp.where(match, order[None, None, :], capacity), axis=2)
    return jnp.concatenate(
        [
            target,
            source,
            term,
            keep,
            last,
            ghost_list[0].reshape(-1),
            lists.reshape(-1),
            rank.reshape(-1),
            cut_axis,
            mig_count[0],
        ]
    )


def kernel(
    at,
    sizes,
    table,
    segments,
    matrix,
    result,
    geo,
    inv,
    own,
    near,
    far,
    terms,
    weights_a,
    weights_b,
    sums,
    field,
    got,
    ghost_out,
    ghost_in,
    inv_out,
    inv_in,
    geo_out,
    geo_in,
    ghost_send,
    ghost_recv,
    inv_send,
    inv_recv,
    geo_send,
    geo_recv,
):
    blocks, tiles, ghosts, capacity = sizes
    width = segments.shape[2]
    here = tuple(lax.axis_index(name) for name in ("gx", "gy", "gz"))

    def shifted(axis, by):
        count = lax.axis_size(("gx", "gy", "gz")[axis])
        place = list(here)
        place[axis] = lax.rem(here[axis] + (by % count), count)
        return tuple(place)

    neighbours = []
    for axis in range(3):
        neighbours += [shifted(axis, 1), shifted(axis, -1)]
    partners = [
        shifted(axis, lax.axis_size(name) // 2) for axis, name in enumerate(("gx", "gy", "gz"))
    ]

    barrier = pltpu.get_barrier_semaphore()
    for device in neighbours + partners:
        pl.semaphore_signal(barrier, inc=1, device_id=device, device_id_type=MESH)

    row = lax.broadcasted_iota(jnp.int32, (8, width), 0)

    def rows(ref, i, count=8):
        return ref[pl.ds(i, count, stride=blocks), :]

    def load_state(i, carry):
        block = segments[i]
        geo[pl.ds(i, 3, stride=blocks), :] = block[0:3]
        geo[pl.ds(3 * blocks + i, 3, stride=blocks), :] = block[6:9]
        inv[pl.ds(i, 3, stride=blocks), :] = block[9:12]
        inv[pl.ds(3 * blocks + i, 3, stride=blocks), :] = block[3:6]
        return carry

    geo[6 * blocks : 8 * blocks, :] = jnp.zeros((2 * blocks, width), jnp.float32)
    inv[6 * blocks : 8 * blocks, :] = jnp.zeros((2 * blocks, width), jnp.float32)
    lax.fori_loop(0, blocks, load_state, 0, unroll=8)
    terms[blocks + ghosts] = jnp.zeros((8, width), jnp.float32)
    sums[tiles] = jnp.zeros((8, width), jnp.float32)
    weights_b[...] = jnp.zeros_like(weights_b)
    pl.semaphore_wait(barrier, 9)

    def products(block):
        first = jnp.where(
            row >= 6, pltpu.roll(block, 3, 0), jnp.where(row == 2, pltpu.roll(block, 7, 0), block)
        )
        second = jnp.where(
            row >= 6, pltpu.roll(block, 2, 0), jnp.where(row == 2, pltpu.roll(block, 5, 0), block)
        )
        second = jnp.where(
            (row >= 3) & (row < 6), block, second
        )
        return first * second

    def features(block, target):
        place = jnp.where(row < 3, block, 0.0)
        square = place * place
        norm = pltpu.roll(square, 3, 0) + pltpu.roll(square, 2, 0) + pltpu.roll(square, 1, 0)
        if target:
            place, norm = -2.0 * place, norm + core_square
        whole = jnp.where(row == 3, norm, place)
        high = whole.astype(jnp.bfloat16).astype(jnp.float32)
        rest = whole - high
        middle = rest.astype(jnp.bfloat16).astype(jnp.float32)
        low = rest - middle
        upper = row < 4
        edge = (row == 3) | (row == 7)
        high_up, middle_up = pltpu.roll(high, 4, 0), pltpu.roll(middle, 4, 0)
        mixed = jnp.where(upper, high, middle_up)
        if target:
            low_up = pltpu.roll(low, 4, 0)
            parts = [
                mixed,
                jnp.where(row == 7, 1.0, jnp.where(upper, low, high_up)),
                jnp.where(edge, 1.0, mixed),
                jnp.where(edge, 0.0, jnp.where(upper, middle, low_up)),
            ]
        else:
            small = jnp.where(upper, low, middle_up)
            parts = [
                jnp.where(edge, 1.0, jnp.where(upper, high, high_up)),
                jnp.where(row == 3, 1.0, mixed),
                jnp.where(row == 7, high_up, small),
                small,
            ]
        return jnp.concatenate(parts, axis=0).astype(jnp.bfloat16)

    def ghost_copy(s, face):
        axis, low = face // 2, face % 2
        octants = ghost_out.at[s]
        bit = 1 - low
        part = (octants.at[bit], octants.at[:, bit], octants.at[:, :, bit])[axis]
        return pltpu.make_async_remote_copy(
            src_ref=part,
            dst_ref=ghost_in.at[s, face],
            send_sem=ghost_send.at[s, face],
            recv_sem=ghost_recv.at[s, face],
            device_id=neighbours[face],
            device_id_type=MESH,
        )

    def partner_copy(source, landing, send, recv, s, axis):
        return pltpu.make_async_remote_copy(
            src_ref=source.at[s],
            dst_ref=landing.at[s, axis],
            send_sem=send.at[s, axis],
            recv_sem=recv.at[s, axis],
            device_id=partners[axis],
            device_id_type=MESH,
        )

    def step(s, carry):
        def own_block(i, c):
            block = jnp.where(row < 3, rows(geo, i), rows(inv, i))
            own[i] = block
            near[i] = features(block, True)
            far[i] = features(block, False).T
            terms[i] = products(block)
            return c

        lax.fori_loop(0, blocks, own_block, 0, unroll=8)

        for o in range(8):
            for q in range(4):
                pick = table[at["ghost"] + o * 4 + q]
                ghost_out[s, o // 4, (o // 2) % 2, o % 2, q] = own[pick]
        for face in range(6):
            ghost_copy(s, face).start()

        my_count = table[at["count"] + s].astype(jnp.float32)

        def out_inv(r, c):
            slot = table[at["mig"] + s * capacity + r]
            inv_out[s, r] = rows(inv, slot)
            return c

        lax.fori_loop(0, capacity, out_inv, 0, unroll=8)
        inv_out[s, capacity] = jnp.full((8, width), my_count, jnp.float32)
        for axis in range(3):
            partner_copy(inv_out, inv_in, inv_send, inv_recv, s, axis).start()

        for face in range(6):
            ghost_copy(s, face).wait_recv()

            def ghost_block(q, c, face=face):
                for u in range(4):
                    block = ghost_in[s, face, q // 2, q % 2, u]
                    spot = blocks + face * 16 + q * 4 + u
                    far[spot] = features(block, False).T
                    terms[spot] = products(block)
                return c

            lax.fori_loop(0, 4, ghost_block, 0, unroll=2)

        def weigh(t, out):
            product = jnp.dot(
                far[table[at["source"] + t]],
                near[table[at["target"] + t]],
                preferred_element_type=jnp.float32,
            )
            out[...] = (1.0 / jnp.maximum(product, core_square)).astype(jnp.bfloat16)

        blank = jnp.zeros((8, width), jnp.float32)

        def add_pair(t, weights, u, run):
            first = terms[table[at["term"] + t]]
            second = terms[table[at["term"] + t + 1]]
            left = jnp.concatenate([first, blank], axis=0)
            right = jnp.concatenate([blank, second], axis=0)
            both = jnp.dot(
                jnp.concatenate([left, right], axis=1).astype(jnp.bfloat16),
                jnp.concatenate([weights[u], weights[u + 1]], axis=0),
                preferred_element_type=jnp.float32,
            )
            for v in range(2):
                run = jnp.where(table[at["keep"] + t + v] != 0, run, 0.0) + both[8 * v : 8 * v + 8]
                sums[t + v] = run
            return run

        groups = tiles // GROUP

        def half(g, run, fill, ready):
            past = lax.rem(g + groups - 1, groups)
            for u in range(0, GROUP, 2):
                for v in range(2):
                    weigh(g * GROUP + u + v, fill.at[u + v])
                run = add_pair(past * GROUP + u, ready, u, run)
            return run

        def two_groups(h, run):
            run = half(2 * h, run, weights_a, weights_b)
            return half(2 * h + 1, run, weights_b, weights_a)

        run = lax.fori_loop(0, groups // 2, two_groups, blank)
        for u in range(0, GROUP, 2):
            run = add_pair((groups - 1) * GROUP + u, weights_b, u, run)

        def collect(i, c):
            field[pl.ds(i, 8, stride=blocks), :] = sums[table[at["last"] + i]]
            return c

        lax.fori_loop(0, blocks, collect, 0, unroll=8)

        def comp(ref, k):
            return ref[k * blocks : (k + 1) * blocks, :]

        scale = stress_coef / width
        sxx, syy, szz = (comp(field, k) * scale for k in (3, 4, 5))
        sxy, syz, sxz = (comp(field, k) * scale for k in (6, 7, 2))
        b = [comp(inv, k) for k in (3, 4, 5)]
        force = (
            sxx * b[0] + sxy * b[1] + sxz * b[2],
            sxy * b[0] + syy * b[1] + syz * b[2],
            sxz * b[0] + syz * b[1] + szz * b[2],
        )
        for k in range(3):
            velocity = comp(inv, k) * force[k]
            previous = comp(geo, 3 + k)
            geo[k * blocks : (k + 1) * blocks, :] = comp(geo, k) + time_step * (
                1.5 * velocity - 0.5 * previous
            )
            geo[(3 + k) * blocks : (4 + k) * blocks, :] = velocity
        geo[0 : 3 * blocks, :] = jnp.dot(
            geo[0 : 3 * blocks, :],
            matrix[...],
            precision=lax.Precision.HIGHEST,
            preferred_element_type=jnp.float32,
        )

        def out_geo(r, c):
            slot = table[at["mig"] + s * capacity + r]
            geo_out[s, r] = rows(geo, slot)
            return c

        lax.fori_loop(0, capacity, out_geo, 0, unroll=8)
        for axis in range(3):
            partner_copy(geo_out, geo_in, geo_send, geo_recv, s, axis).start()
        for axis in range(3):
            partner_copy(inv_out, inv_in, inv_send, inv_recv, s, axis).wait_recv()
        cut = table[at["cut"] + s]

        def chosen(landing, r):
            later = jnp.where(cut == 1, landing[s, 1, r], landing[s, 2, r])
            return jnp.where(cut == 0, landing[s, 0, r], later)

        limit = jnp.minimum(chosen(inv_in, capacity), my_count)

        def take(ref, landing):
            def gather(r, c):
                got[r] = chosen(landing, r)
                return c

            lax.fori_loop(0, capacity, gather, 0, unroll=8)

            def body(i, c):
                r = table[at["rank"] + s * blocks + i]
                arrived = got[jnp.minimum(r, capacity - 1)]
                live = limit > r.astype(jnp.float32)
                ref[pl.ds(i, 8, stride=blocks), :] = jnp.where(live, arrived, rows(ref, i))
                return c

            lax.fori_loop(0, blocks, body, 0, unroll=8)

        take(inv, inv_in)
        for axis in range(3):
            partner_copy(geo_out, geo_in, geo_send, geo_recv, s, axis).wait_recv()
        take(geo, geo_in)
        for face in range(6):
            ghost_copy(s, face).wait_send()
        for axis in range(3):
            partner_copy(inv_out, inv_in, inv_send, inv_recv, s, axis).wait_send()
            partner_copy(geo_out, geo_in, geo_send, geo_recv, s, axis).wait_send()
        return carry

    lax.fori_loop(0, STEPS, step, 0)

    def store_state(i, carry):
        g, v = rows(geo, i), rows(inv, i)
        result[i, 0:3, :] = g[0:3]
        result[i, 3:6, :] = v[3:6]
        result[i, 6:9, :] = g[3:6]
        result[i, 9:12, :] = v[0:3]
        return carry

    lax.fori_loop(0, blocks, store_state, 0, unroll=8)


def on_device(
    segments, remesh_matrix, ghost_list, pair_list, tile_count, cut_axis, mig_list, mig_count
):
    blocks, _, width = segments.shape
    tiles = pair_list.shape[1]
    per_cell = ghost_list.shape[2]
    ghosts = 24 * per_cell
    capacity = mig_list.shape[2]
    at, _ = layout_of(tiles, blocks, 8 * per_cell, capacity)
    table = index_table(
        ghost_list, pair_list, tile_count, cut_axis, mig_list, mig_count, blocks, blocks + ghosts
    )
    vmem = pl.BlockSpec(memory_space=pltpu.VMEM)
    f32, bf16 = jnp.float32, jnp.bfloat16
    return pl.pallas_call(
        functools.partial(kernel, at, (blocks, tiles, ghosts, capacity)),
        out_shape=jax.ShapeDtypeStruct(segments.shape, f32),
        in_specs=[pl.BlockSpec(memory_space=pltpu.SMEM), vmem, vmem],
        out_specs=vmem,
        scratch_shapes=[
            pltpu.VMEM((8 * blocks, width), f32),
            pltpu.VMEM((8 * blocks, width), f32),
            pltpu.VMEM((blocks, 8, width), f32),
            pltpu.VMEM((blocks, 32, width), bf16),
            pltpu.VMEM((blocks + ghosts, width, 32), bf16),
            pltpu.VMEM((blocks + ghosts + 1, 8, width), f32),
            pltpu.VMEM((GROUP, width, width), bf16),
            pltpu.VMEM((GROUP, width, width), bf16),
            pltpu.VMEM((tiles + 1, 8, width), f32),
            pltpu.VMEM((8 * blocks, width), f32),
            pltpu.VMEM((capacity, 8, width), f32),
            pltpu.VMEM((STEPS, 2, 2, 2, per_cell, 8, width), f32),
            pltpu.VMEM((STEPS, 6, 2, 2, per_cell, 8, width), f32),
            pltpu.VMEM((STEPS, capacity + 1, 8, width), f32),
            pltpu.VMEM((STEPS, 3, capacity + 1, 8, width), f32),
            pltpu.VMEM((STEPS, capacity, 8, width), f32),
            pltpu.VMEM((STEPS, 3, capacity, 8, width), f32),
            pltpu.SemaphoreType.DMA((STEPS, 6)),
            pltpu.SemaphoreType.DMA((STEPS, 6)),
            pltpu.SemaphoreType.DMA((STEPS, 3)),
            pltpu.SemaphoreType.DMA((STEPS, 3)),
            pltpu.SemaphoreType.DMA((STEPS, 3)),
            pltpu.SemaphoreType.DMA((STEPS, 3)),
        ],
        compiler_params=pltpu.CompilerParams(
            collective_id=0, has_side_effects=True, vmem_limit_bytes=48 * 1024 * 1024
        ),
    )(table, segments, remesh_matrix)


def solution(mesh):
    return jax.shard_map(
        on_device,
        mesh=mesh,
        in_specs=(
            P(("gx", "gy", "gz"), None, None),
            P(),
            P(("gx", "gy", "gz"), None, None),
            P(("gx", "gy", "gz"), None, None),
            P(("gx", "gy", "gz")),
            P(),
            P(("gx", "gy", "gz"), None, None),
            P(("gx", "gy", "gz"), None),
        ),
        out_specs=P(("gx", "gy", "gz"), None, None),
        check_vma=False,
    )
```

```python
import functools

import jax
import jax.numpy as jnp
from jax import lax
from jax.experimental import pallas as pl
from jax.experimental.pallas import tpu as pltpu
from jax.sharding import PartitionSpec as P

STEPS = 3
MESH = pl.DeviceIdType.MESH

core_square = 0.1
time_step = 0.5
stress_coef = 0.25

GROUP = 16


def layout_of(tiles, blocks, ghosts, slots):
    sizes = dict(
        target=tiles,
        source=tiles,
        term=tiles,
        keep=tiles,
        last=blocks,
        ghost=ghosts,
        mig=STEPS * slots,
        rank=STEPS * blocks,
        cut=STEPS,
        count=STEPS,
    )
    offsets, total = {}, 0
    for name, size in sizes.items():
        offsets[name] = total
        total += size
    return offsets, total


def index_table(ghost_list, pair_list, tile_count, cut_axis, mig_list, mig_count, blocks, ghosts):
    tiles = pair_list.shape[1]
    lists = mig_list[0]
    capacity = lists.shape[1]
    targets, origin = pair_list[0, :, 0], pair_list[0, :, 1]
    number = jnp.arange(tiles, dtype=jnp.int32)
    dead = (number >= tile_count[0]).astype(jnp.int32)
    key = targets * tiles + number
    place = jnp.sum((key[None, :] < key[:, None]).astype(jnp.int32), axis=1)
    packed = (targets * 1024 + origin) * 2 + dead
    hit = place[None, :] == number[:, None]
    ordered = jnp.sum(jnp.where(hit, packed[None, :], 0), axis=1)
    target = ordered // 2048
    source = (ordered // 2) % 1024
    source = jnp.where(source < blocks, source, source + capacity)
    term = jnp.where(ordered % 2 == 1, blocks + capacity + ghosts, source)
    before = jnp.concatenate([jnp.full((1,), -1, jnp.int32), target[:-1]])
    keep = (target == before).astype(jnp.int32)
    slot = jnp.arange(blocks, dtype=jnp.int32)
    upto = jnp.sum((targets[None, :] <= slot[:, None]).astype(jnp.int32), axis=1)
    own = jnp.sum((targets[None, :] == slot[:, None]).astype(jnp.int32), axis=1)
    last = jnp.where(own > 0, upto - 1, tiles)
    match = lists[:, None, :] == slot[None, :, None]
    order = jnp.arange(capacity, dtype=jnp.int32)
    rank = jnp.min(jnp.where(match, order[None, None, :], capacity), axis=2)
    return jnp.concatenate(
        [
            target,
            source,
            term,
            keep,
            last,
            ghost_list[0].reshape(-1),
            lists.reshape(-1),
            rank.reshape(-1),
            cut_axis,
            mig_count[0],
        ]
    )


def kernel(
    at,
    sizes,
    table,
    segments,
    matrix,
    result,
    geo,
    inv,
    own,
    near,
    far,
    terms,
    weights_a,
    weights_b,
    sums,
    field,
    remap,
    counts,
    count_out,
    count_in,
    ghost_out,
    ghost_in,
    inv_out,
    inv_in,
    pos_out,
    pos_in,
    vel_out,
    vel_in,
    inv_got,
    pos_got,
    vel_got,
    count_local,
    count_send,
    count_recv,
    ghost_send,
    ghost_recv,
    inv_send,
    inv_recv,
    pos_send,
    pos_recv,
    vel_send,
    vel_recv,
):
    blocks, tiles, ghosts, capacity = sizes
    width = segments.shape[2]
    held = blocks + capacity
    here = tuple(lax.axis_index(name) for name in ("gx", "gy", "gz"))

    def shifted(axis, by):
        count = lax.axis_size(("gx", "gy", "gz")[axis])
        place = list(here)
        place[axis] = lax.rem(here[axis] + (by % count), count)
        return tuple(place)

    neighbours = []
    for axis in range(3):
        neighbours += [shifted(axis, 1), shifted(axis, -1)]
    partners = [
        shifted(axis, lax.axis_size(name) // 2) for axis, name in enumerate(("gx", "gy", "gz"))
    ]

    barrier = pltpu.get_barrier_semaphore()
    for device in neighbours + partners:
        pl.semaphore_signal(barrier, inc=1, device_id=device, device_id_type=MESH)

    row = lax.broadcasted_iota(jnp.int32, (8, width), 0)
    blank = jnp.zeros((8, width), jnp.float32)

    def rows(ref, i, stride=blocks, count=8):
        return ref[pl.ds(i, count, stride=stride), :]

    def remote(source, landing, send, recv, device):
        return pltpu.make_async_remote_copy(
            src_ref=source,
            dst_ref=landing,
            send_sem=send,
            recv_sem=recv,
            device_id=device,
            device_id_type=MESH,
        )

    def load_state(i, carry):
        block = segments[i]
        geo[pl.ds(i, 3, stride=blocks), :] = block[0:3]
        geo[pl.ds(3 * blocks + i, 3, stride=blocks), :] = block[6:9]
        inv[pl.ds(i, 3, stride=blocks), :] = block[9:12]
        inv[pl.ds(3 * blocks + i, 3, stride=blocks), :] = block[3:6]
        own[i] = block[0:8]
        return carry

    geo[6 * blocks : 8 * blocks, :] = jnp.zeros((2 * blocks, width), jnp.float32)
    inv[6 * blocks : 8 * blocks, :] = jnp.zeros((2 * blocks, width), jnp.float32)
    lax.fori_loop(0, blocks, load_state, 0, unroll=8)
    terms[held + ghosts] = blank
    sums[tiles] = blank
    weights_b[...] = jnp.zeros_like(weights_b)
    for ref in (inv_got, pos_got, vel_got):
        ref[...] = jnp.zeros_like(ref)

    def plain(i, carry):
        remap[i] = i
        return carry

    lax.fori_loop(0, held + ghosts + 1, plain, 0)
    for s in range(STEPS):
        count_out[s] = jnp.full((8, width), table[at["count"] + s], jnp.int32)
    pl.semaphore_wait(barrier, 9)

    def products(block):
        first = jnp.where(
            row >= 6, pltpu.roll(block, 3, 0), jnp.where(row == 2, pltpu.roll(block, 7, 0), block)
        )
        second = jnp.where(
            row >= 6, pltpu.roll(block, 2, 0), jnp.where(row == 2, pltpu.roll(block, 5, 0), block)
        )
        return first * second

    def features(block, target):
        place = jnp.where(row < 3, block, 0.0)
        square = place * place
        norm = pltpu.roll(square, 3, 0) + pltpu.roll(square, 2, 0) + pltpu.roll(square, 1, 0)
        if target:
            place, norm = -2.0 * place, norm + core_square
        whole = jnp.where(row == 3, norm, place)
        high = whole.astype(jnp.bfloat16).astype(jnp.float32)
        rest = whole - high
        middle = rest.astype(jnp.bfloat16).astype(jnp.float32)
        low = rest - middle
        upper = row < 4
        edge = (row == 3) | (row == 7)
        high_up, middle_up = pltpu.roll(high, 4, 0), pltpu.roll(middle, 4, 0)
        mixed = jnp.where(upper, high, middle_up)
        if target:
            low_up = pltpu.roll(low, 4, 0)
            parts = [
                mixed,
                jnp.where(row == 7, 1.0, jnp.where(upper, low, high_up)),
                jnp.where(edge, 1.0, mixed),
                jnp.where(edge, 0.0, jnp.where(upper, middle, low_up)),
            ]
        else:
            small = jnp.where(upper, low, middle_up)
            parts = [
                jnp.where(edge, 1.0, jnp.where(upper, high, high_up)),
                jnp.where(row == 3, 1.0, mixed),
                jnp.where(row == 7, high_up, small),
                small,
            ]
        return jnp.concatenate(parts, axis=0).astype(jnp.bfloat16)

    def prepare(i, block, target):
        if target:
            near[i] = features(block, True)
        far[i] = features(block, False).T
        terms[i] = products(block)

    def prepare_own(i, c):
        prepare(i, own[i], True)
        return c

    def ghost_copy(s, face):
        axis, low = face // 2, face % 2
        octants = ghost_out.at[s]
        bit = 1 - low
        part = (octants.at[bit], octants.at[:, bit], octants.at[:, :, bit])[axis]
        return remote(
            part,
            ghost_in.at[s, face],
            ghost_send.at[s, face],
            ghost_recv.at[s, face],
            neighbours[face],
        )

    def partner_copy(kind, s, axis):
        source, landing, send, recv, parts = kind
        span = pl.ds(0, parts * capacity)
        return remote(
            source.at[s, span],
            landing.at[s, axis, span],
            send.at[s, axis],
            recv.at[s, axis],
            partners[axis],
        )

    moved_inv = (inv_out, inv_in, inv_send, inv_recv, 6)
    moved_pos = (pos_out, pos_in, pos_send, pos_recv, 3)
    moved_vel = (vel_out, vel_in, vel_send, vel_recv, 3)

    def count_copy(axis):
        return remote(
            count_out, count_in.at[axis], count_send.at[axis], count_recv.at[axis], partners[axis]
        )

    def collect_arrivals(kind, got, s):
        landing, parts = kind[1], kind[4]
        cut = table[at["cut"] + s]
        first, second = cut == 0, cut == 1
        for k in range(parts * capacity // 8):
            span = pl.ds(8 * k, 8)
            later = jnp.where(second, landing[s, 1, span], landing[s, 2, span])
            got[span] = jnp.where(first, landing[s, 0, span], later)

    def limit_of(s):
        return jnp.minimum(table[at["count"] + s], counts[table[at["cut"] + s], s, 0, 0])

    def ghost_gather(s):
        for o in range(8):
            for q in range(4):
                pick = remap[table[at["ghost"] + o * 4 + q]]
                ghost_out[s, o // 4, (o // 2) % 2, o % 2, q] = own[pick]

    def weigh(t, out):
        product = jnp.dot(
            far[remap[table[at["source"] + t]]],
            near[remap[table[at["target"] + t]]],
            preferred_element_type=jnp.float32,
        )
        out[...] = (1.0 / jnp.maximum(product, core_square)).astype(jnp.bfloat16)

    def add_pair(t, weights, u, run):
        first = terms[remap[table[at["term"] + t]]]
        second = terms[remap[table[at["term"] + t + 1]]]
        left = jnp.concatenate([first, blank], axis=0)
        right = jnp.concatenate([blank, second], axis=0)
        both = jnp.dot(
            jnp.concatenate([left, right], axis=1).astype(jnp.bfloat16),
            jnp.concatenate([weights[u], weights[u + 1]], axis=0),
            preferred_element_type=jnp.float32,
        )
        for v in range(2):
            run = jnp.where(table[at["keep"] + t + v] != 0, run, 0.0) + both[8 * v : 8 * v + 8]
            sums[t + v] = run
        return run

    groups = tiles // GROUP

    def half(g, run, fill, ready):
        past = lax.rem(g + groups - 1, groups)
        for u in range(0, GROUP, 2):
            for v in range(2):
                weigh(g * GROUP + u + v, fill.at[u + v])
            run = add_pair(past * GROUP + u, ready, u, run)
        return run

    def two_groups(h, run):
        run = half(2 * h, run, weights_a, weights_b)
        return half(2 * h + 1, run, weights_b, weights_a)

    def collect(i, c):
        field[pl.ds(i, 8, stride=blocks), :] = sums[table[at["last"] + i]]
        return c

    def comp(ref, k):
        return ref[k * blocks : (k + 1) * blocks, :]

    def settle(s, pieces):
        limit = limit_of(s)

        def body(i, c):
            r = table[at["rank"] + s * blocks + i]
            spot = jnp.minimum(r, capacity - 1)
            for ref, base, got, parts in pieces:
                span = pl.ds(base * blocks + i, parts, stride=blocks)
                arrived = rows(got, spot, capacity, parts)
                ref[span, :] = jnp.where(r < limit, arrived, ref[span, :])
            return c

        lax.fori_loop(0, blocks, body, 0, unroll=8)

    placed = ((geo, 0, pos_got, 3), (inv, 0, inv_got, 6))

    def advance():
        scale = stress_coef / width
        sxx, syy, szz = (comp(field, k) * scale for k in (3, 4, 5))
        sxy, syz, sxz = (comp(field, k) * scale for k in (6, 7, 2))
        b = [comp(inv, k) for k in (3, 4, 5)]
        force = (
            sxx * b[0] + sxy * b[1] + sxz * b[2],
            sxy * b[0] + syy * b[1] + syz * b[2],
            sxz * b[0] + syz * b[1] + szz * b[2],
        )
        for k in range(3):
            velocity = comp(inv, k) * force[k]
            previous = comp(geo, 3 + k)
            geo[k * blocks : (k + 1) * blocks, :] = comp(geo, k) + time_step * (
                1.5 * velocity - 0.5 * previous
            )
            geo[(3 + k) * blocks : (4 + k) * blocks, :] = velocity
        geo[0 : 3 * blocks, :] = jnp.dot(
            geo[0 : 3 * blocks, :],
            matrix[...],
            precision=lax.Precision.HIGHEST,
            preferred_element_type=jnp.float32,
        )

    def gather_out(s, outs):
        def body(r, c):
            slot = table[at["mig"] + s * capacity + r]
            for ref, base, out, parts in outs:
                block = ref[pl.ds(base * blocks + slot, parts, stride=blocks), :]
                out[s, pl.ds(r, parts, stride=capacity), :] = block
            return c

        lax.fori_loop(0, capacity, body, 0, unroll=8)

    for axis in range(3):
        count_copy(axis).start()

    def step(s, carry):
        ghost_gather(s)
        for face in range(6):
            ghost_copy(s, face).start()

        @pl.when(s == 0)
        def _():
            lax.fori_loop(0, blocks, prepare_own, 0, unroll=8)
            for axis in range(3):
                count_copy(axis).wait_recv()
            local = pltpu.make_async_copy(count_in, counts, count_local)
            local.start()
            local.wait()

        @pl.when(s > 0)
        def _():
            settle(s - 1, placed)

            def prepare_arrived(r, c):
                prepare(blocks + r, own[blocks + r], True)
                return c

            lax.fori_loop(0, capacity, prepare_arrived, 0, unroll=8)

        gather_out(s, ((inv, 0, inv_out, 6),))
        for face in range(6):
            ghost_copy(s, face).wait_recv()

            def ghost_block(q, c, face=face):
                for u in range(4):
                    spot = held + face * 16 + q * 4 + u
                    prepare(spot, ghost_in[s, face, q // 2, q % 2, u], False)
                return c

            lax.fori_loop(0, 4, ghost_block, 0, unroll=2)
        for axis in range(3):
            partner_copy(moved_inv, s, axis).start()

        @pl.when(s > 0)
        def _():
            for axis in range(3):
                partner_copy(moved_vel, s - 1, axis).start()

        run = lax.fori_loop(0, groups // 2, two_groups, blank)
        for u in range(0, GROUP, 2):
            run = add_pair((groups - 1) * GROUP + u, weights_b, u, run)
        lax.fori_loop(0, blocks, collect, 0, unroll=8)

        @pl.when(s > 0)
        def _():
            for axis in range(3):
                partner_copy(moved_vel, s - 1, axis).wait_recv()
            collect_arrivals(moved_vel, vel_got, s - 1)
            settle(s - 1, ((geo, 3, vel_got, 3),))

        advance()
        gather_out(s, ((geo, 0, pos_out, 3), (geo, 3, vel_out, 3)))
        for axis in range(3):
            partner_copy(moved_pos, s, axis).start()

        @pl.when(s == STEPS - 1)
        def _():
            for axis in range(3):
                partner_copy(moved_vel, s, axis).start()

        @pl.when(s < STEPS - 1)
        def _():
            def rebuild(i, c):
                block = jnp.where(row < 3, rows(geo, i), rows(inv, i))
                own[i] = block
                prepare(i, block, True)
                return c

            lax.fori_loop(0, blocks, rebuild, 0, unroll=8)

        limit = limit_of(s)

        def route(i, c):
            r = table[at["rank"] + s * blocks + i]
            remap[i] = jnp.where(r < limit, blocks + r, i)
            return c

        lax.fori_loop(0, blocks, route, 0, unroll=8)
        for axis in range(3):
            partner_copy(moved_inv, s, axis).wait_recv()
        collect_arrivals(moved_inv, inv_got, s)
        for axis in range(3):
            partner_copy(moved_pos, s, axis).wait_recv()
        collect_arrivals(moved_pos, pos_got, s)

        @pl.when(s < STEPS - 1)
        def _():
            def arrive(r, c):
                place = rows(pos_got, r, capacity)
                own[blocks + r] = jnp.where(row < 3, place, rows(inv_got, r, capacity))
                return c

            lax.fori_loop(0, capacity, arrive, 0, unroll=8)

        for face in range(6):
            ghost_copy(s, face).wait_send()
        for axis in range(3):
            partner_copy(moved_inv, s, axis).wait_send()
            partner_copy(moved_pos, s, axis).wait_send()
        return carry

    lax.fori_loop(0, STEPS, step, 0)
    last = STEPS - 1
    settle(last, placed)
    for axis in range(3):
        partner_copy(moved_vel, last, axis).wait_recv()
    collect_arrivals(moved_vel, vel_got, last)
    settle(last, ((geo, 3, vel_got, 3),))

    def store_state(i, carry):
        g, v = rows(geo, i), rows(inv, i)
        result[i, 0:3, :] = g[0:3]
        result[i, 3:6, :] = v[3:6]
        result[i, 6:9, :] = g[3:6]
        result[i, 9:12, :] = v[0:3]
        return carry

    lax.fori_loop(0, blocks, store_state, 0, unroll=8)
    for axis in range(3):
        count_copy(axis).wait_send()
        for s in range(STEPS):
            partner_copy(moved_vel, s, axis).wait_send()


def on_device(
    segments, remesh_matrix, ghost_list, pair_list, tile_count, cut_axis, mig_list, mig_count
):
    blocks, _, width = segments.shape
    tiles = pair_list.shape[1]
    per_cell = ghost_list.shape[2]
    ghosts = 24 * per_cell
    capacity = mig_list.shape[2]
    at, _ = layout_of(tiles, blocks, 8 * per_cell, capacity)
    table = index_table(
        ghost_list, pair_list, tile_count, cut_axis, mig_list, mig_count, blocks, ghosts
    )
    vmem = pl.BlockSpec(memory_space=pltpu.VMEM)
    f32, bf16 = jnp.float32, jnp.bfloat16
    held = blocks + capacity
    return pl.pallas_call(
        functools.partial(kernel, at, (blocks, tiles, ghosts, capacity)),
        out_shape=jax.ShapeDtypeStruct(segments.shape, f32),
        in_specs=[pl.BlockSpec(memory_space=pltpu.SMEM), vmem, vmem],
        out_specs=vmem,
        scratch_shapes=[
            pltpu.VMEM((8 * blocks, width), f32),
            pltpu.VMEM((8 * blocks, width), f32),
            pltpu.VMEM((held, 8, width), f32),
            pltpu.VMEM((held, 32, width), bf16),
            pltpu.VMEM((held + ghosts, width, 32), bf16),
            pltpu.VMEM((held + ghosts + 1, 8, width), f32),
            pltpu.VMEM((GROUP, width, width), bf16),
            pltpu.VMEM((GROUP, width, width), bf16),
            pltpu.VMEM((tiles + 1, 8, width), f32),
            pltpu.VMEM((8 * blocks, width), f32),
            pltpu.SMEM((held + ghosts + 1,), jnp.int32),
            pltpu.SMEM((3, STEPS, 8, width), jnp.int32),
            pltpu.VMEM((STEPS, 8, width), jnp.int32),
            pltpu.VMEM((3, STEPS, 8, width), jnp.int32),
            pltpu.VMEM((STEPS, 2, 2, 2, per_cell, 8, width), f32),
            pltpu.VMEM((STEPS, 6, 2, 2, per_cell, 8, width), f32),
            pltpu.VMEM((STEPS, 8 * capacity, width), f32),
            pltpu.VMEM((STEPS, 3, 8 * capacity, width), f32),
            pltpu.VMEM((STEPS, 8 * capacity, width), f32),
            pltpu.VMEM((STEPS, 3, 8 * capacity, width), f32),
            pltpu.VMEM((STEPS, 8 * capacity, width), f32),
            pltpu.VMEM((STEPS, 3, 8 * capacity, width), f32),
            pltpu.VMEM((8 * capacity, width), f32),
            pltpu.VMEM((8 * capacity, width), f32),
            pltpu.VMEM((8 * capacity, width), f32),
            pltpu.SemaphoreType.DMA,
            pltpu.SemaphoreType.DMA((3,)),
            pltpu.SemaphoreType.DMA((3,)),
            pltpu.SemaphoreType.DMA((STEPS, 6)),
            pltpu.SemaphoreType.DMA((STEPS, 6)),
            pltpu.SemaphoreType.DMA((STEPS, 3)),
            pltpu.SemaphoreType.DMA((STEPS, 3)),
            pltpu.SemaphoreType.DMA((STEPS, 3)),
            pltpu.SemaphoreType.DMA((STEPS, 3)),
            pltpu.SemaphoreType.DMA((STEPS, 3)),
            pltpu.SemaphoreType.DMA((STEPS, 3)),
        ],
        compiler_params=pltpu.CompilerParams(
            collective_id=0, has_side_effects=True, vmem_limit_bytes=48 * 1024 * 1024
        ),
    )(table, segments, remesh_matrix)


def solution(mesh):
    return jax.shard_map(
        on_device,
        mesh=mesh,
        in_specs=(
            P(("gx", "gy", "gz"), None, None),
            P(),
            P(("gx", "gy", "gz"), None, None),
            P(("gx", "gy", "gz"), None, None),
            P(("gx", "gy", "gz")),
            P(),
            P(("gx", "gy", "gz"), None, None),
            P(("gx", "gy", "gz"), None),
        ),
        out_specs=P(("gx", "gy", "gz"), None, None),
        check_vma=False,
    )
```

```python
import functools

import jax
import jax.numpy as jnp
from jax import lax
from jax.experimental import pallas as pl
from jax.experimental.pallas import tpu as pltpu
from jax.sharding import PartitionSpec as P

STEPS = 3
MESH = pl.DeviceIdType.MESH

core_square = 0.1
time_step = 0.5
stress_coef = 0.25

GROUP = 32


def layout_of(tiles, blocks, ghosts, slots):
    sizes = dict(
        target=tiles,
        source=tiles,
        term=tiles,
        keep=tiles,
        last=blocks,
        ghost=ghosts,
        mig=STEPS * slots,
        rank=STEPS * blocks,
        cut=STEPS,
        count=STEPS,
    )
    offsets, total = {}, 0
    for name, size in sizes.items():
        offsets[name] = total
        total += size
    return offsets, total


def index_table(ghost_list, pair_list, tile_count, cut_axis, mig_list, mig_count, blocks, ghosts):
    tiles = pair_list.shape[1]
    lists = mig_list[0]
    capacity = lists.shape[1]
    targets, origin = pair_list[0, :, 0], pair_list[0, :, 1]
    number = jnp.arange(tiles, dtype=jnp.int32)
    dead = (number >= tile_count[0]).astype(jnp.int32)
    key = targets * tiles + number
    place = jnp.sum((key[None, :] < key[:, None]).astype(jnp.int32), axis=1)
    packed = (targets * 1024 + origin) * 2 + dead
    hit = place[None, :] == number[:, None]
    ordered = jnp.sum(jnp.where(hit, packed[None, :], 0), axis=1)
    target = ordered // 2048
    source = (ordered // 2) % 1024
    source = jnp.where(source < blocks, source, source + capacity)
    term = jnp.where(ordered % 2 == 1, blocks + capacity + ghosts, source)
    before = jnp.concatenate([jnp.full((1,), -1, jnp.int32), target[:-1]])
    keep = (target == before).astype(jnp.int32)
    slot = jnp.arange(blocks, dtype=jnp.int32)
    upto = jnp.sum((targets[None, :] <= slot[:, None]).astype(jnp.int32), axis=1)
    own = jnp.sum((targets[None, :] == slot[:, None]).astype(jnp.int32), axis=1)
    last = jnp.where(own > 0, upto - 1, tiles)
    match = lists[:, None, :] == slot[None, :, None]
    order = jnp.arange(capacity, dtype=jnp.int32)
    rank = jnp.min(jnp.where(match, order[None, None, :], capacity), axis=2)
    return jnp.concatenate(
        [
            target,
            source,
            term,
            keep,
            last,
            ghost_list[0].reshape(-1),
            lists.reshape(-1),
            rank.reshape(-1),
            cut_axis,
            mig_count[0],
        ]
    )


def kernel(
    at,
    sizes,
    table,
    segments,
    matrix,
    result,
    geo,
    inv,
    own_pos,
    own_b,
    near,
    far,
    terms,
    weights_a,
    weights_b,
    sums,
    field,
    remap,
    counts,
    count_out,
    count_in,
    gpos_out,
    gpos_in,
    gb_out,
    gb_in,
    inv_out,
    inv_in,
    pos_out,
    pos_in,
    vel_out,
    vel_in,
    inv_got,
    pos_got,
    vel_got,
    count_local,
    count_send,
    count_recv,
    gpos_send,
    gpos_recv,
    gb_send,
    gb_recv,
    inv_send,
    inv_recv,
    pos_send,
    pos_recv,
    vel_send,
    vel_recv,
):
    blocks, tiles, ghosts, capacity = sizes
    width = segments.shape[2]
    held = blocks + capacity
    here = tuple(lax.axis_index(name) for name in ("gx", "gy", "gz"))

    def shifted(axis, by):
        count = lax.axis_size(("gx", "gy", "gz")[axis])
        place = list(here)
        place[axis] = lax.rem(here[axis] + (by % count), count)
        return tuple(place)

    neighbours = []
    for axis in range(3):
        neighbours += [shifted(axis, 1), shifted(axis, -1)]
    partners = [
        shifted(axis, lax.axis_size(name) // 2) for axis, name in enumerate(("gx", "gy", "gz"))
    ]

    barrier = pltpu.get_barrier_semaphore()
    for device in neighbours + partners:
        pl.semaphore_signal(barrier, inc=1, device_id=device, device_id_type=MESH)

    row = lax.broadcasted_iota(jnp.int32, (8, width), 0)
    upper = row < 4
    edge = (row == 3) | (row == 7)
    blank = jnp.zeros((8, width), jnp.float32)
    half_core = 0.5 * core_square

    def rows(ref, i, stride=blocks, count=8):
        return ref[pl.ds(i, count, stride=stride), :]

    def remote(source, landing, send, recv, device):
        return pltpu.make_async_remote_copy(
            src_ref=source,
            dst_ref=landing,
            send_sem=send,
            recv_sem=recv,
            device_id=device,
            device_id_type=MESH,
        )

    def load_state(i, carry):
        block = segments[i]
        geo[pl.ds(i, 3, stride=blocks), :] = block[0:3]
        geo[pl.ds(4 * blocks + i, 3, stride=blocks), :] = block[6:9]
        inv[pl.ds(i, 3, stride=blocks), :] = block[3:6]
        inv[pl.ds(4 * blocks + i, 3, stride=blocks), :] = block[9:12]
        place = block[0:8]
        square = place * place
        norm = pltpu.roll(square, 3, 0) + pltpu.roll(square, 2, 0) + pltpu.roll(square, 1, 0)
        own_pos[i] = jnp.where(row < 3, place, norm + half_core)
        own_b[i] = pltpu.roll(place, 5, 0)
        return carry

    for ref in (geo, inv):
        for k in (3, 7):
            ref[k * blocks : (k + 1) * blocks, :] = jnp.zeros((blocks, width), jnp.float32)
    lax.fori_loop(0, blocks, load_state, 0, unroll=8)
    terms[held + ghosts] = blank
    sums[tiles] = blank
    weights_b[...] = jnp.zeros_like(weights_b)
    for ref in (inv_got, pos_got, vel_got):
        ref[...] = jnp.zeros_like(ref)

    def plain(i, carry):
        remap[i] = i
        return carry

    lax.fori_loop(0, held + ghosts + 1, plain, 0)
    for s in range(STEPS):
        count_out[s] = jnp.full((8, width), table[at["count"] + s], jnp.int32)
    pl.semaphore_wait(barrier, 9)

    def joined(first, second):
        return jnp.where(upper, first, pltpu.roll(second, 4, 0))

    def products(pair):
        once, twice = pair * pltpu.roll(pair, 7, 0), pair * pltpu.roll(pair, 6, 0)
        square = pair * pair
        first = jnp.where(row == 3, pltpu.roll(twice, 3, 0), pltpu.roll(once, 4, 0))
        second = jnp.where(row == 3, pltpu.roll(twice, 7, 0), once)
        return (
            jnp.where(row < 3, square, first),
            jnp.where(row < 3, pltpu.roll(square, 4, 0), second),
        )

    def features(pair, i, target):
        high = pair.astype(jnp.bfloat16).astype(jnp.float32)
        rest = pair - high
        middle = rest.astype(jnp.bfloat16).astype(jnp.float32)
        parts = (high, middle, rest - middle)
        turned = tuple(pltpu.roll(part, 4, 0) for part in parts)
        factor = jnp.where(edge, 1.0, -2.0)
        for v, (up, down) in enumerate(((parts, turned), (turned, parts))):
            mixed = jnp.where(upper, up[0], down[1])
            small = jnp.where(upper, up[2], down[1])
            stack = [
                jnp.where(edge, 1.0, jnp.where(upper, up[0], down[0])),
                jnp.where(row == 3, 1.0, mixed),
                jnp.where(row == 7, down[0], small),
                small,
            ]
            far[i + v] = jnp.concatenate(stack, axis=0).astype(jnp.bfloat16).T
            if target:
                stack = [
                    factor * mixed,
                    jnp.where(row == 7, 1.0, factor * jnp.where(upper, up[2], down[0])),
                    jnp.where(edge, 1.0, factor * mixed),
                    jnp.where(edge, 0.0, factor * jnp.where(upper, up[1], down[2])),
                ]
                near[i + v] = jnp.concatenate(stack, axis=0).astype(jnp.bfloat16)

    def prepare_own(h, c):
        i = 2 * h
        features(joined(own_pos[i], own_pos[i + 1]), i, True)
        terms[i], terms[i + 1] = products(joined(own_b[i], own_b[i + 1]))
        return c

    def ghost_copy(kind, s, face):
        source, landing, send, recv = kind
        axis, low = face // 2, face % 2
        octants = source.at[s]
        bit = 1 - low
        part = (octants.at[bit], octants.at[:, bit], octants.at[:, :, bit])[axis]
        return remote(
            part, landing.at[s, face], send.at[s, face], recv.at[s, face], neighbours[face]
        )

    ghost_pos = (gpos_out, gpos_in, gpos_send, gpos_recv)
    ghost_b = (gb_out, gb_in, gb_send, gb_recv)

    def ghost_gather(kind, table_of, s):
        for o in range(8):
            for h in range(2):
                base = at["ghost"] + o * 4 + 2 * h
                first, second = table_of[remap[table[base]]], table_of[remap[table[base + 1]]]
                kind[0][s, o // 4, (o // 2) % 2, o % 2, h] = joined(first, second)
        for face in range(6):
            ghost_copy(kind, s, face).start()

    def partner_copy(kind, s, axis):
        source, landing, send, recv, parts = kind
        span = pl.ds(0, parts * capacity)
        return remote(
            source.at[s, span],
            landing.at[s, axis, span],
            send.at[s, axis],
            recv.at[s, axis],
            partners[axis],
        )

    moved_inv = (inv_out, inv_in, inv_send, inv_recv, 6)
    moved_pos = (pos_out, pos_in, pos_send, pos_recv, 3)
    moved_vel = (vel_out, vel_in, vel_send, vel_recv, 3)

    def count_copy(axis):
        return remote(
            count_out, count_in.at[axis], count_send.at[axis], count_recv.at[axis], partners[axis]
        )

    def collect_arrivals(kind, got, s):
        landing, parts = kind[1], kind[4]
        cut = table[at["cut"] + s]
        first, second = cut == 0, cut == 1
        for k in range(parts * capacity // 8):
            span = pl.ds(8 * k, 8)
            later = jnp.where(second, landing[s, 1, span], landing[s, 2, span])
            got[span] = jnp.where(first, landing[s, 0, span], later)

    def limit_of(s):
        return jnp.minimum(table[at["count"] + s], counts[table[at["cut"] + s], s, 0, 0])

    def weigh(t, out):
        product = jnp.dot(
            far[remap[table[at["source"] + t]]],
            near[remap[table[at["target"] + t]]],
            preferred_element_type=jnp.float32,
        )
        out[...] = (1.0 / jnp.maximum(product, core_square)).astype(jnp.bfloat16)

    def add_pair(t, weights, u, run):
        first = terms[remap[table[at["term"] + t]]]
        second = terms[remap[table[at["term"] + t + 1]]]
        left = jnp.concatenate([first, blank], axis=0)
        right = jnp.concatenate([blank, second], axis=0)
        both = jnp.dot(
            jnp.concatenate([left, right], axis=1).astype(jnp.bfloat16),
            jnp.concatenate([weights[u], weights[u + 1]], axis=0),
            preferred_element_type=jnp.float32,
        )
        for v in range(2):
            run = jnp.where(table[at["keep"] + t + v] != 0, run, 0.0) + both[8 * v : 8 * v + 8]
            sums[t + v] = run
        return run

    groups = tiles // GROUP

    def half(g, run, fill, ready):
        past = lax.rem(g + groups - 1, groups)
        for u in range(0, GROUP, 2):
            for v in range(2):
                weigh(g * GROUP + u + v, fill.at[u + v])
            run = add_pair(past * GROUP + u, ready, u, run)
        return run

    def two_groups(h, run):
        run = half(2 * h, run, weights_a, weights_b)
        return half(2 * h + 1, run, weights_b, weights_a)

    def collect(i, c):
        field[pl.ds(i, 8, stride=blocks), :] = sums[table[at["last"] + i]]
        return c

    def comp(ref, k):
        return ref[k * blocks : (k + 1) * blocks, :]

    def settle(s, pieces):
        limit = limit_of(s)

        def body(i, c):
            r = table[at["rank"] + s * blocks + i]
            spot = jnp.minimum(r, capacity - 1)
            for ref, base, got, first, parts in pieces:
                span = pl.ds(base * blocks + i, parts, stride=blocks)
                arrived = rows(got, first * capacity + spot, capacity, parts)
                ref[span, :] = jnp.where(r < limit, arrived, ref[span, :])
            return c

        lax.fori_loop(0, blocks, body, 0, unroll=8)

    placed = ((geo, 0, pos_got, 0, 3), (inv, 0, inv_got, 0, 3), (inv, 4, inv_got, 3, 3))

    def norm_of(ref, count):
        x, y, z = (ref[k * count : (k + 1) * count, :] for k in range(3))
        return x * x + y * y + z * z + half_core

    def advance():
        scale = stress_coef / width
        sxx, syy, szz = (comp(field, k) * scale for k in (0, 1, 2))
        sxy, syz, sxz = (comp(field, k) * scale for k in (4, 5, 3))
        b = [comp(inv, k) for k in (0, 1, 2)]
        force = (
            sxx * b[0] + sxy * b[1] + sxz * b[2],
            sxy * b[0] + syy * b[1] + syz * b[2],
            sxz * b[0] + syz * b[1] + szz * b[2],
        )
        for k in range(3):
            velocity = comp(inv, 4 + k) * force[k]
            previous = comp(geo, 4 + k)
            geo[k * blocks : (k + 1) * blocks, :] = comp(geo, k) + time_step * (
                1.5 * velocity - 0.5 * previous
            )
            geo[(4 + k) * blocks : (5 + k) * blocks, :] = velocity
        geo[0 : 3 * blocks, :] = jnp.dot(
            geo[0 : 3 * blocks, :],
            matrix[...],
            precision=lax.Precision.HIGHEST,
            preferred_element_type=jnp.float32,
        )
        geo[3 * blocks : 4 * blocks, :] = norm_of(geo, blocks)

    def gather_out(s, outs):
        def body(r, c):
            slot = table[at["mig"] + s * capacity + r]
            for ref, base, out, first, parts in outs:
                block = ref[pl.ds(base * blocks + slot, parts, stride=blocks), :]
                out[s, pl.ds(first * capacity + r, parts, stride=capacity), :] = block
            return c

        lax.fori_loop(0, capacity, body, 0, unroll=8)

    for axis in range(3):
        count_copy(axis).start()
    ghost_gather(ghost_b, own_b, 0)

    def step(s, carry):
        ghost_gather(ghost_pos, own_pos, s)

        @pl.when(s == 0)
        def _():
            lax.fori_loop(0, blocks // 2, prepare_own, 0, unroll=8)
            for axis in range(3):
                count_copy(axis).wait_recv()
            local = pltpu.make_async_copy(count_in, counts, count_local)
            local.start()
            local.wait()

        @pl.when(s > 0)
        def _():
            lax.fori_loop(blocks // 2, held // 2, prepare_own, 0, unroll=6)
            settle(s - 1, placed)

        gather_out(s, ((inv, 0, inv_out, 0, 3), (inv, 4, inv_out, 3, 3)))
        for face in range(6):
            ghost_copy(ghost_b, s, face).wait_recv()

        def ghost_terms(face, c):
            for k in range(8):
                spot = held + face * 16 + 2 * k
                pair = gb_in[s, face, k // 4, (k // 2) % 2, k % 2]
                terms[spot], terms[spot + 1] = products(pair)
            return c

        lax.fori_loop(0, 6, ghost_terms, 0, unroll=2)
        for face in range(6):
            ghost_copy(ghost_pos, s, face).wait_recv()

        def ghost_features(face, c):
            for k in range(8):
                spot = held + face * 16 + 2 * k
                features(gpos_in[s, face, k // 4, (k // 2) % 2, k % 2], spot, False)
            return c

        lax.fori_loop(0, 6, ghost_features, 0, unroll=2)
        for axis in range(3):
            partner_copy(moved_inv, s, axis).start()

        @pl.when(s > 0)
        def _():
            for axis in range(3):
                partner_copy(moved_vel, s - 1, axis).start()

        run = lax.fori_loop(0, groups // 2, two_groups, blank)
        for u in range(0, GROUP, 2):
            run = add_pair((groups - 1) * GROUP + u, weights_b, u, run)
        lax.fori_loop(0, blocks, collect, 0, unroll=8)

        @pl.when(s > 0)
        def _():
            for axis in range(3):
                partner_copy(moved_vel, s - 1, axis).wait_recv()
            collect_arrivals(moved_vel, vel_got, s - 1)
            settle(s - 1, ((geo, 4, vel_got, 0, 3),))

        advance()
        gather_out(s, ((geo, 0, pos_out, 0, 3),))
        for axis in range(3):
            partner_copy(moved_pos, s, axis).start()
        gather_out(s, ((geo, 4, vel_out, 0, 3),))

        @pl.when(s == STEPS - 1)
        def _():
            for axis in range(3):
                partner_copy(moved_vel, s, axis).start()

        for axis in range(3):
            partner_copy(moved_inv, s, axis).wait_recv()
        collect_arrivals(moved_inv, inv_got, s)

        @pl.when(s < STEPS - 1)
        def _():
            limit = limit_of(s)

            def route(i, c):
                r = table[at["rank"] + s * blocks + i]
                remap[i] = jnp.where(r < limit, blocks + r, i)
                return c

            lax.fori_loop(0, blocks, route, 0, unroll=8)

            def arrive_b(r, c):
                own_b[blocks + r] = rows(inv_got, r, capacity)
                return c

            def refresh(i, c):
                own_pos[i] = rows(geo, i)
                own_b[i] = rows(inv, i)
                return c

            lax.fori_loop(0, capacity, arrive_b, 0, unroll=8)
            lax.fori_loop(0, blocks, refresh, 0, unroll=8)
            ghost_gather(ghost_b, own_b, s + 1)
            lax.fori_loop(0, blocks // 2, prepare_own, 0, unroll=8)

        for axis in range(3):
            partner_copy(moved_pos, s, axis).wait_recv()
        collect_arrivals(moved_pos, pos_got, s)

        @pl.when(s < STEPS - 1)
        def _():
            pos_got[3 * capacity : 4 * capacity, :] = norm_of(pos_got, capacity)

            def arrive(r, c):
                own_pos[blocks + r] = rows(pos_got, r, capacity)
                return c

            lax.fori_loop(0, capacity, arrive, 0, unroll=8)

        for face in range(6):
            ghost_copy(ghost_b, s, face).wait_send()
            ghost_copy(ghost_pos, s, face).wait_send()
        for axis in range(3):
            partner_copy(moved_inv, s, axis).wait_send()
            partner_copy(moved_pos, s, axis).wait_send()
        return carry

    lax.fori_loop(0, STEPS, step, 0)
    last = STEPS - 1
    settle(last, placed)
    for axis in range(3):
        partner_copy(moved_vel, last, axis).wait_recv()
    collect_arrivals(moved_vel, vel_got, last)
    settle(last, ((geo, 4, vel_got, 0, 3),))

    def store_state(i, carry):
        g, v = rows(geo, i), rows(inv, i)
        result[i, 0:3, :] = g[0:3]
        result[i, 3:6, :] = v[0:3]
        result[i, 6:9, :] = g[4:7]
        result[i, 9:12, :] = v[4:7]
        return carry

    lax.fori_loop(0, blocks, store_state, 0, unroll=8)
    for axis in range(3):
        count_copy(axis).wait_send()
        for s in range(STEPS):
            partner_copy(moved_vel, s, axis).wait_send()


def on_device(
    segments, remesh_matrix, ghost_list, pair_list, tile_count, cut_axis, mig_list, mig_count
):
    blocks, _, width = segments.shape
    tiles = pair_list.shape[1]
    per_cell = ghost_list.shape[2]
    ghosts = 24 * per_cell
    capacity = mig_list.shape[2]
    at, _ = layout_of(tiles, blocks, 8 * per_cell, capacity)
    table = index_table(
        ghost_list, pair_list, tile_count, cut_axis, mig_list, mig_count, blocks, ghosts
    )
    vmem = pl.BlockSpec(memory_space=pltpu.VMEM)
    f32, bf16 = jnp.float32, jnp.bfloat16
    held = blocks + capacity
    return pl.pallas_call(
        functools.partial(kernel, at, (blocks, tiles, ghosts, capacity)),
        out_shape=jax.ShapeDtypeStruct(segments.shape, f32),
        in_specs=[pl.BlockSpec(memory_space=pltpu.SMEM), vmem, vmem],
        out_specs=vmem,
        scratch_shapes=[
            pltpu.VMEM((8 * blocks, width), f32),
            pltpu.VMEM((8 * blocks, width), f32),
            pltpu.VMEM((held, 8, width), f32),
            pltpu.VMEM((held, 8, width), f32),
            pltpu.VMEM((held, 32, width), bf16),
            pltpu.VMEM((held + ghosts, width, 32), bf16),
            pltpu.VMEM((held + ghosts + 1, 8, width), f32),
            pltpu.VMEM((GROUP, width, width), bf16),
            pltpu.VMEM((GROUP, width, width), bf16),
            pltpu.VMEM((tiles + 1, 8, width), f32),
            pltpu.VMEM((8 * blocks, width), f32),
            pltpu.SMEM((held + ghosts + 1,), jnp.int32),
            pltpu.SMEM((3, STEPS, 8, width), jnp.int32),
            pltpu.VMEM((STEPS, 8, width), jnp.int32),
            pltpu.VMEM((3, STEPS, 8, width), jnp.int32),
            pltpu.VMEM((STEPS, 2, 2, 2, per_cell // 2, 8, width), f32),
            pltpu.VMEM((STEPS, 6, 2, 2, per_cell // 2, 8, width), f32),
            pltpu.VMEM((STEPS, 2, 2, 2, per_cell // 2, 8, width), f32),
            pltpu.VMEM((STEPS, 6, 2, 2, per_cell // 2, 8, width), f32),
            pltpu.VMEM((STEPS, 8 * capacity, width), f32),
            pltpu.VMEM((STEPS, 3, 8 * capacity, width), f32),
            pltpu.VMEM((STEPS, 8 * capacity, width), f32),
            pltpu.VMEM((STEPS, 3, 8 * capacity, width), f32),
            pltpu.VMEM((STEPS, 8 * capacity, width), f32),
            pltpu.VMEM((STEPS, 3, 8 * capacity, width), f32),
            pltpu.VMEM((8 * capacity, width), f32),
            pltpu.VMEM((8 * capacity, width), f32),
            pltpu.VMEM((8 * capacity, width), f32),
            pltpu.SemaphoreType.DMA,
            pltpu.SemaphoreType.DMA((3,)),
            pltpu.SemaphoreType.DMA((3,)),
            pltpu.SemaphoreType.DMA((STEPS, 6)),
            pltpu.SemaphoreType.DMA((STEPS, 6)),
            pltpu.SemaphoreType.DMA((STEPS, 6)),
            pltpu.SemaphoreType.DMA((STEPS, 6)),
            pltpu.SemaphoreType.DMA((STEPS, 3)),
            pltpu.SemaphoreType.DMA((STEPS, 3)),
            pltpu.SemaphoreType.DMA((STEPS, 3)),
            pltpu.SemaphoreType.DMA((STEPS, 3)),
            pltpu.SemaphoreType.DMA((STEPS, 3)),
            pltpu.SemaphoreType.DMA((STEPS, 3)),
        ],
        compiler_params=pltpu.CompilerParams(
            collective_id=0, has_side_effects=True, vmem_limit_bytes=48 * 1024 * 1024
        ),
    )(table, segments, remesh_matrix)


def solution(mesh):
    return jax.shard_map(
        on_device,
        mesh=mesh,
        in_specs=(
            P(("gx", "gy", "gz"), None, None),
            P(),
            P(("gx", "gy", "gz"), None, None),
            P(("gx", "gy", "gz"), None, None),
            P(("gx", "gy", "gz")),
            P(),
            P(("gx", "gy", "gz"), None, None),
            P(("gx", "gy", "gz"), None),
        ),
        out_specs=P(("gx", "gy", "gz"), None, None),
        check_vma=False,
    )
```

```python
import functools

import jax
import jax.numpy as jnp
from jax import lax
from jax.experimental import pallas as pl
from jax.experimental.pallas import tpu as pltpu
from jax.sharding import PartitionSpec as P

STEPS = 3
MESH = pl.DeviceIdType.MESH

core_square = 0.1
time_step = 0.5
stress_coef = 0.25

GROUP = 32


TARGET, SOURCE, TERM, KEEP, LAST, RANK = 0, 4, 8, 12, 16, 17


def kernel(
    sizes,
    pairs,
    used,
    ghost_list,
    cuts,
    lists,
    amounts,
    segments,
    remesh,
    result,
    geo,
    inv,
    matrix,
    draft,
    table,
    own_pos,
    own_b,
    near,
    far,
    terms,
    weights_a,
    weights_b,
    sums,
    field,
    remap,
    counts,
    count_out,
    count_in,
    gpos_out,
    gpos_in,
    gb_out,
    gb_in,
    inv_out,
    inv_in,
    pos_out,
    pos_in,
    vel_out,
    vel_in,
    inv_got,
    pos_got,
    vel_got,
    load_sems,
    count_local,
    count_send,
    count_recv,
    gpos_send,
    gpos_recv,
    gb_send,
    gb_recv,
    inv_send,
    inv_recv,
    pos_send,
    pos_recv,
    vel_send,
    vel_recv,
):
    blocks, tiles, ghosts, capacity = sizes
    width = segments.shape[1]
    held = blocks + capacity
    here = tuple(lax.axis_index(name) for name in ("gx", "gy", "gz"))

    def shifted(axis, by):
        count = lax.axis_size(("gx", "gy", "gz")[axis])
        place = list(here)
        place[axis] = lax.rem(here[axis] + (by % count), count)
        return tuple(place)

    neighbours = []
    for axis in range(3):
        neighbours += [shifted(axis, 1), shifted(axis, -1)]
    partners = [
        shifted(axis, lax.axis_size(name) // 2) for axis, name in enumerate(("gx", "gy", "gz"))
    ]

    barrier = pltpu.get_barrier_semaphore()
    for device in neighbours + partners:
        pl.semaphore_signal(barrier, inc=1, device_id=device, device_id_type=MESH)

    row = lax.broadcasted_iota(jnp.int32, (8, width), 0)
    upper = row < 4
    edge = (row == 3) | (row == 7)
    blank = jnp.zeros((8, width), jnp.float32)
    half_core = 0.5 * core_square

    def rows(ref, i, stride=blocks, count=8):
        return ref[pl.ds(i, count, stride=stride), :]

    def remote(source, landing, send, recv, device):
        return pltpu.make_async_remote_copy(
            src_ref=source,
            dst_ref=landing,
            send_sem=send,
            recv_sem=recv,
            device_id=device,
            device_id_type=MESH,
        )

    loads = (
        (segments.at[pl.ds(0, 3 * blocks)], geo.at[pl.ds(0, 3 * blocks)]),
        (segments.at[pl.ds(3 * blocks, 3 * blocks)], inv.at[pl.ds(0, 3 * blocks)]),
        (segments.at[pl.ds(6 * blocks, 3 * blocks)], geo.at[pl.ds(4 * blocks, 3 * blocks)]),
        (segments.at[pl.ds(9 * blocks, 3 * blocks)], inv.at[pl.ds(4 * blocks, 3 * blocks)]),
        (remesh, matrix),
    )
    loads = [
        pltpu.make_async_copy(source, landing, load_sems.at[k])
        for k, (source, landing) in enumerate(loads)
    ]
    for load in loads:
        load.start()
    for ref in (geo, inv):
        for k in (3, 7):
            ref[k * blocks : (k + 1) * blocks, :] = jnp.zeros((blocks, width), jnp.float32)
    terms[held + ghosts] = blank
    sums[tiles] = blank
    weights_b[...] = jnp.zeros_like(weights_b)
    for ref in (inv_got, pos_got, vel_got):
        ref[...] = jnp.zeros_like(ref)

    def plain(i, carry):
        remap[i] = i
        return carry

    lax.fori_loop(0, held + ghosts + 1, plain, 0, unroll=37)
    for s in range(STEPS):
        count_out[s : s + 1, :] = jnp.full((1, width), amounts[0, s], jnp.int32)

    def joined(first, second):
        return jnp.where(upper, first, pltpu.roll(second, 4, 0))

    def products(pair):
        once, twice = pair * pltpu.roll(pair, 7, 0), pair * pltpu.roll(pair, 6, 0)
        square = pair * pair
        first = jnp.where(row == 3, pltpu.roll(twice, 3, 0), pltpu.roll(once, 4, 0))
        second = jnp.where(row == 3, pltpu.roll(twice, 7, 0), once)
        return (
            jnp.where(row < 3, square, first),
            jnp.where(row < 3, pltpu.roll(square, 4, 0), second),
        )

    def features(pair, i, target):
        high = pair.astype(jnp.bfloat16).astype(jnp.float32)
        rest = pair - high
        middle = rest.astype(jnp.bfloat16).astype(jnp.float32)
        parts = (high, middle, rest - middle)
        turned = tuple(pltpu.roll(part, 4, 0) for part in parts)
        factor = jnp.where(edge, 1.0, -2.0)
        for v, (up, down) in enumerate(((parts, turned), (turned, parts))):
            mixed = jnp.where(upper, up[0], down[1])
            small = jnp.where(upper, up[2], down[1])
            stack = [
                jnp.where(edge, 1.0, jnp.where(upper, up[0], down[0])),
                jnp.where(row == 3, 1.0, mixed),
                jnp.where(row == 7, down[0], small),
                small,
            ]
            far[i + v] = jnp.concatenate(stack, axis=0).astype(jnp.bfloat16).T
            if target:
                stack = [
                    factor * mixed,
                    jnp.where(row == 7, 1.0, factor * jnp.where(upper, up[2], down[0])),
                    jnp.where(edge, 1.0, factor * mixed),
                    jnp.where(edge, 0.0, factor * jnp.where(upper, up[1], down[2])),
                ]
                near[i + v] = jnp.concatenate(stack, axis=0).astype(jnp.bfloat16)

    def prepare_own(h, c):
        i = 2 * h
        features(joined(own_pos[i], own_pos[i + 1]), i, True)
        terms[i], terms[i + 1] = products(joined(own_b[i], own_b[i + 1]))
        return c

    def ghost_copy(kind, s, face):
        source, landing, send, recv = kind
        axis, low = face // 2, face % 2
        octants = source.at[s]
        bit = 1 - low
        part = (octants.at[bit], octants.at[:, bit], octants.at[:, :, bit])[axis]
        return remote(
            part, landing.at[s, face], send.at[s, face], recv.at[s, face], neighbours[face]
        )

    ghost_pos = (gpos_out, gpos_in, gpos_send, gpos_recv)
    ghost_b = (gb_out, gb_in, gb_send, gb_recv)

    def ghost_gather(kind, block_of, s):
        for o in range(8):
            for h in range(2):
                first = block_of(remap[ghost_list[2 * h, o]])
                second = block_of(remap[ghost_list[2 * h + 1, o]])
                kind[0][s, o // 4, (o // 2) % 2, o % 2, h] = joined(first, second)
        for face in range(6):
            ghost_copy(kind, s, face).start()

    def note(line, values):
        draft[pl.ds(line * width, width)] = values[0]

    def order_pairs():
        number = lax.broadcasted_iota(jnp.int32, (1, tiles), 1)
        lane = lax.broadcasted_iota(jnp.int32, (1, width), 1)
        key = pairs[0:1, :] * tiles + number
        dead = jnp.where(number >= used[0], 1, 0)
        packed = (pairs[0:1, :] * 1024 + pairs[1:2, :]) * 2 + dead
        columns = jnp.concatenate([key, packed, jnp.zeros((6, tiles), jnp.int32)], axis=0).T
        ordered = jnp.zeros((1, tiles), jnp.int32)
        upto, before = jnp.zeros((1, width), jnp.int32), jnp.zeros((1, width), jnp.int32)
        for c in range(0, tiles, width):
            column = columns[c : c + width, 0:1]
            place = jnp.sum(jnp.where(key < column, 1, 0), axis=1, keepdims=True)
            content = columns[c : c + width, 1:2]
            ordered += jnp.sum(jnp.where(place == number, content, 0), axis=0, keepdims=True)
            upto += jnp.sum(
                jnp.where(column < (lane + 1) * tiles, 1, 0), axis=0, keepdims=True
            )
            before += jnp.sum(jnp.where(column < lane * tiles, 1, 0), axis=0, keepdims=True)
        source = lax.shift_right_logical(ordered, 1) & 1023
        source = jnp.where(source < blocks, source, source + capacity)
        target = lax.shift_right_logical(ordered, 11)
        prior = pltpu.roll(jnp.broadcast_to(target, (8, tiles)), 1, 1)[0:1]
        term = jnp.where((ordered & 1) == 1, held + ghosts, source)
        keep = jnp.where((target == prior) & (number > 0), 1, 0)
        for c in range(tiles // width):
            for part, values in ((TARGET, target), (SOURCE, source), (TERM, term), (KEEP, keep)):
                note(part + c, values[:, c * width : (c + 1) * width])
        note(LAST, jnp.where(upto > before, upto - 1, tiles))
        for s in range(STEPS):
            rank = jnp.full((1, width), capacity, jnp.int32)
            for r in range(capacity):
                rank = jnp.where(lane == lists[s, 0, r], r, rank)
            note(RANK + s, rank)

    def partner_copy(kind, s, axis):
        source, landing, send, recv, parts = kind
        span = pl.ds(0, parts * capacity)
        return remote(
            source.at[s, span],
            landing.at[s, axis, span],
            send.at[s, axis],
            recv.at[s, axis],
            partners[axis],
        )

    moved_inv = (inv_out, inv_in, inv_send, inv_recv, 6)
    moved_pos = (pos_out, pos_in, pos_send, pos_recv, 3)
    moved_vel = (vel_out, vel_in, vel_send, vel_recv, 3)

    def count_copy(axis):
        return remote(
            count_out, count_in.at[axis], count_send.at[axis], count_recv.at[axis], partners[axis]
        )

    def collect_arrivals(kind, got, s):
        landing, parts = kind[1], kind[4]
        cut = cuts[s]
        first, second = cut == 0, cut == 1
        for k in range(parts * capacity // 8):
            span = pl.ds(8 * k, 8)
            later = jnp.where(second, landing[s, 1, span], landing[s, 2, span])
            got[span] = jnp.where(first, landing[s, 0, span], later)

    def limit_of(s):
        return jnp.minimum(amounts[0, s], counts[cuts[s], s, 0])

    def entry(part, spot, u):
        return table[spot + (part * width + u)]

    def weigh(spot, u, out):
        product = jnp.dot(
            far[remap[entry(SOURCE, spot, u)]],
            near[remap[entry(TARGET, spot, u)]],
            preferred_element_type=jnp.float32,
        )
        out[...] = (1.0 / jnp.maximum(product, core_square)).astype(jnp.bfloat16)

    def add_pair(t, spot, weights, u, run):
        first = terms[remap[entry(TERM, spot, u)]]
        second = terms[remap[entry(TERM, spot, u + 1)]]
        left = jnp.concatenate([first, blank], axis=0)
        right = jnp.concatenate([blank, second], axis=0)
        both = jnp.dot(
            jnp.concatenate([left, right], axis=1).astype(jnp.bfloat16),
            jnp.concatenate([weights[u], weights[u + 1]], axis=0),
            preferred_element_type=jnp.float32,
        )
        for v in range(2):
            run = jnp.where(entry(KEEP, spot, u + v) != 0, run, 0.0) + both[8 * v : 8 * v + 8]
            sums[t + u + v] = run
        return run

    def spot_of(g):
        return g * GROUP

    groups = tiles // GROUP

    def half(g, run, fill, ready):
        past = lax.rem(g + groups - 1, groups)
        spot, before = spot_of(g), spot_of(past)
        for u in range(0, GROUP, 2):
            for v in range(2):
                weigh(spot, u + v, fill.at[u + v])
            run = add_pair(past * GROUP, before, ready, u, run)
        return run

    def two_groups(h, run):
        run = half(2 * h, run, weights_a, weights_b)
        return half(2 * h + 1, run, weights_b, weights_a)

    def collect(i, c):
        field[pl.ds(i, 8, stride=blocks), :] = sums[table[LAST * width + i]]
        return c

    def comp(ref, k):
        return ref[k * blocks : (k + 1) * blocks, :]

    def settle(s, pieces):
        limit = limit_of(s)

        def body(i, c):
            r = table[(RANK + s) * width + i]
            spot = jnp.minimum(r, capacity - 1)
            for ref, base, got, first, parts, *target in pieces:
                span = pl.ds(base * blocks + i, parts, stride=blocks)
                arrived = rows(got, first * capacity + spot, capacity, parts)
                fresh = jnp.where(r < limit, arrived, ref[span, :])
                if target:
                    out, at = target
                    out[pl.ds(at * blocks + i, parts, stride=blocks), :] = fresh
                else:
                    ref[span, :] = fresh
            return c

        lax.fori_loop(0, blocks, body, 0, unroll=8)

    placed = ((geo, 0, pos_got, 0, 3), (inv, 0, inv_got, 0, 3), (inv, 4, inv_got, 3, 3))

    def norm_of(ref, count):
        x, y, z = (ref[k * count : (k + 1) * count, :] for k in range(3))
        return x * x + y * y + z * z + half_core

    def advance():
        scale = stress_coef / width
        sxx, syy, szz = (comp(field, k) * scale for k in (0, 1, 2))
        sxy, syz, sxz = (comp(field, k) * scale for k in (4, 5, 3))
        b = [comp(inv, k) for k in (0, 1, 2)]
        force = (
            sxx * b[0] + sxy * b[1] + sxz * b[2],
            sxy * b[0] + syy * b[1] + syz * b[2],
            sxz * b[0] + syz * b[1] + szz * b[2],
        )
        for k in range(3):
            velocity = comp(inv, 4 + k) * force[k]
            previous = comp(geo, 4 + k)
            geo[k * blocks : (k + 1) * blocks, :] = comp(geo, k) + time_step * (
                1.5 * velocity - 0.5 * previous
            )
            geo[(4 + k) * blocks : (5 + k) * blocks, :] = velocity
        geo[0 : 3 * blocks, :] = jnp.dot(
            geo[0 : 3 * blocks, :],
            matrix[...],
            precision=lax.Precision.HIGHEST,
            preferred_element_type=jnp.float32,
        )
        geo[3 * blocks : 4 * blocks, :] = norm_of(geo, blocks)

    def gather_out(s, outs):
        def body(r, c):
            slot = lists[s, 0, r]
            for ref, base, out, first, parts in outs:
                block = ref[pl.ds(base * blocks + slot, parts, stride=blocks), :]
                out[s, pl.ds(first * capacity + r, parts, stride=capacity), :] = block
            return c

        lax.fori_loop(0, capacity, body, 0, unroll=8)

    for load in loads[:4]:
        load.wait()
    geo[3 * blocks : 4 * blocks, :] = norm_of(geo, blocks)
    pl.semaphore_wait(barrier, 9)
    ghost_gather(ghost_pos, lambda pick: rows(geo, pick), 0)
    ghost_gather(ghost_b, lambda pick: rows(inv, pick), 0)
    for axis in range(3):
        count_copy(axis).start()
    order_pairs()
    ordering = pltpu.make_async_copy(draft, table, load_sems.at[5])
    ordering.start()
    for load in loads[4:]:
        load.wait()

    def refresh(i, c):
        own_pos[i] = rows(geo, i)
        own_b[i] = rows(inv, i)
        return c

    lax.fori_loop(0, blocks, refresh, 0, unroll=8)
    lax.fori_loop(0, blocks // 2, prepare_own, 0, unroll=8)
    for axis in range(3):
        count_copy(axis).wait_recv()
    local = pltpu.make_async_copy(count_in, counts, count_local)
    local.start()
    local.wait()
    ordering.wait()

    def step(s, carry):
        @pl.when(s > 0)
        def _():
            lax.fori_loop(blocks // 2, held // 2, prepare_own, 0, unroll=6)
            settle(s - 1, placed)

        gather_out(s, ((inv, 0, inv_out, 0, 3), (inv, 4, inv_out, 3, 3)))
        for face in range(6):
            ghost_copy(ghost_b, s, face).wait_recv()

        def ghost_terms(face, c):
            for k in range(8):
                spot = held + face * 16 + 2 * k
                pair = gb_in[s, face, k // 4, (k // 2) % 2, k % 2]
                terms[spot], terms[spot + 1] = products(pair)
            return c

        lax.fori_loop(0, 6, ghost_terms, 0, unroll=2)
        for face in range(6):
            ghost_copy(ghost_pos, s, face).wait_recv()

        def ghost_features(face, c):
            for k in range(8):
                spot = held + face * 16 + 2 * k
                features(gpos_in[s, face, k // 4, (k // 2) % 2, k % 2], spot, False)
            return c

        lax.fori_loop(0, 6, ghost_features, 0, unroll=2)
        for axis in range(3):
            partner_copy(moved_inv, s, axis).start()

        @pl.when(s > 0)
        def _():
            for axis in range(3):
                partner_copy(moved_vel, s - 1, axis).start()

        run = lax.fori_loop(0, groups // 2, two_groups, blank)
        for u in range(0, GROUP, 2):
            run = add_pair((groups - 1) * GROUP, spot_of(jnp.int32(groups - 1)), weights_b, u, run)
        lax.fori_loop(0, blocks, collect, 0, unroll=8)

        @pl.when(s > 0)
        def _():
            for axis in range(3):
                partner_copy(moved_vel, s - 1, axis).wait_recv()
            collect_arrivals(moved_vel, vel_got, s - 1)
            settle(s - 1, ((geo, 4, vel_got, 0, 3),))

        advance()
        gather_out(s, ((geo, 0, pos_out, 0, 3),))
        for axis in range(3):
            partner_copy(moved_pos, s, axis).start()
        gather_out(s, ((geo, 4, vel_out, 0, 3),))

        @pl.when(s == STEPS - 1)
        def _():
            for axis in range(3):
                partner_copy(moved_vel, s, axis).start()

        for axis in range(3):
            partner_copy(moved_inv, s, axis).wait_recv()
        collect_arrivals(moved_inv, inv_got, s)

        @pl.when(s < STEPS - 1)
        def _():
            limit = limit_of(s)

            def route(i, c):
                r = table[(RANK + s) * width + i]
                remap[i] = jnp.where(r < limit, blocks + r, i)
                return c

            lax.fori_loop(0, blocks, route, 0, unroll=8)

            def arrive_b(r, c):
                own_b[blocks + r] = rows(inv_got, r, capacity)
                return c

            lax.fori_loop(0, capacity, arrive_b, 0, unroll=8)
            lax.fori_loop(0, blocks, refresh, 0, unroll=8)
            ghost_gather(ghost_b, lambda pick: own_b[pick], s + 1)
            lax.fori_loop(0, blocks // 2, prepare_own, 0, unroll=8)

        @pl.when(s == STEPS - 1)
        def _():
            final = ((inv, 0, inv_got, 0, 3, result, 3), (inv, 4, inv_got, 3, 3, result, 9))
            settle(s, final)

        for axis in range(3):
            partner_copy(moved_pos, s, axis).wait_recv()
        collect_arrivals(moved_pos, pos_got, s)

        @pl.when(s < STEPS - 1)
        def _():
            pos_got[3 * capacity : 4 * capacity, :] = norm_of(pos_got, capacity)

            def arrive(r, c):
                own_pos[blocks + r] = rows(pos_got, r, capacity)
                return c

            lax.fori_loop(0, capacity, arrive, 0, unroll=8)
            ghost_gather(ghost_pos, lambda pick: own_pos[pick], s + 1)

        for face in range(6):
            ghost_copy(ghost_b, s, face).wait_send()
            ghost_copy(ghost_pos, s, face).wait_send()
        for axis in range(3):
            partner_copy(moved_inv, s, axis).wait_send()
            partner_copy(moved_pos, s, axis).wait_send()
        return carry

    lax.fori_loop(0, STEPS, step, 0)
    last = STEPS - 1
    settle(last, ((geo, 0, pos_got, 0, 3, result, 0),))
    for axis in range(3):
        partner_copy(moved_vel, last, axis).wait_recv()
    collect_arrivals(moved_vel, vel_got, last)
    settle(last, ((geo, 4, vel_got, 0, 3, result, 6),))
    for axis in range(3):
        count_copy(axis).wait_send()
        for s in range(STEPS):
            partner_copy(moved_vel, s, axis).wait_send()


def on_device(
    segments, remesh_matrix, ghost_list, pair_list, tile_count, cut_axis, mig_list, mig_count
):
    blocks, _, width = segments.shape
    tiles = pair_list.shape[1]
    per_cell = ghost_list.shape[2]
    ghosts = 24 * per_cell
    capacity = mig_list.shape[2]
    vmem, smem = (pl.BlockSpec(memory_space=m) for m in (pltpu.VMEM, pltpu.SMEM))
    f32, bf16 = jnp.float32, jnp.bfloat16
    held = blocks + capacity
    result = pl.pallas_call(
        functools.partial(kernel, (blocks, tiles, ghosts, capacity)),
        out_shape=jax.ShapeDtypeStruct((12 * blocks, width), f32),
        in_specs=[vmem] + [smem] * 5 + [pl.BlockSpec(memory_space=pltpu.HBM)] * 2,
        out_specs=vmem,
        scratch_shapes=[
            pltpu.VMEM((8 * blocks, width), f32),
            pltpu.VMEM((8 * blocks, width), f32),
            pltpu.VMEM((width, width), f32),
            pltpu.VMEM((24 * width,), jnp.int32),
            pltpu.SMEM((24 * width,), jnp.int32),
            pltpu.VMEM((held, 8, width), f32),
            pltpu.VMEM((held, 8, width), f32),
            pltpu.VMEM((held, 32, width), bf16),
            pltpu.VMEM((held + ghosts, width, 32), bf16),
            pltpu.VMEM((held + ghosts + 1, 8, width), f32),
            pltpu.VMEM((GROUP, width, width), bf16),
            pltpu.VMEM((GROUP, width, width), bf16),
            pltpu.VMEM((tiles + 1, 8, width), f32),
            pltpu.VMEM((8 * blocks, width), f32),
            pltpu.SMEM((held + ghosts + 1,), jnp.int32),
            pltpu.SMEM((3, 8, width), jnp.int32),
            pltpu.VMEM((8, width), jnp.int32),
            pltpu.VMEM((3, 8, width), jnp.int32),
            pltpu.VMEM((STEPS, 2, 2, 2, per_cell // 2, 8, width), f32),
            pltpu.VMEM((STEPS, 6, 2, 2, per_cell // 2, 8, width), f32),
            pltpu.VMEM((STEPS, 2, 2, 2, per_cell // 2, 8, width), f32),
            pltpu.VMEM((STEPS, 6, 2, 2, per_cell // 2, 8, width), f32),
            pltpu.VMEM((STEPS, 8 * capacity, width), f32),
            pltpu.VMEM((STEPS, 3, 8 * capacity, width), f32),
            pltpu.VMEM((STEPS, 8 * capacity, width), f32),
            pltpu.VMEM((STEPS, 3, 8 * capacity, width), f32),
            pltpu.VMEM((STEPS, 8 * capacity, width), f32),
            pltpu.VMEM((STEPS, 3, 8 * capacity, width), f32),
            pltpu.VMEM((8 * capacity, width), f32),
            pltpu.VMEM((8 * capacity, width), f32),
            pltpu.VMEM((8 * capacity, width), f32),
            pltpu.SemaphoreType.DMA((6,)),
            pltpu.SemaphoreType.DMA,
            pltpu.SemaphoreType.DMA((3,)),
            pltpu.SemaphoreType.DMA((3,)),
            pltpu.SemaphoreType.DMA((STEPS, 6)),
            pltpu.SemaphoreType.DMA((STEPS, 6)),
            pltpu.SemaphoreType.DMA((STEPS, 6)),
            pltpu.SemaphoreType.DMA((STEPS, 6)),
            pltpu.SemaphoreType.DMA((STEPS, 3)),
            pltpu.SemaphoreType.DMA((STEPS, 3)),
            pltpu.SemaphoreType.DMA((STEPS, 3)),
            pltpu.SemaphoreType.DMA((STEPS, 3)),
            pltpu.SemaphoreType.DMA((STEPS, 3)),
            pltpu.SemaphoreType.DMA((STEPS, 3)),
        ],
        compiler_params=pltpu.CompilerParams(
            collective_id=0, has_side_effects=True, vmem_limit_bytes=63 * 1024 * 1024
        ),
    )(
        pair_list[0].T,
        tile_count,
        ghost_list[0].T,
        cut_axis,
        jnp.transpose(mig_list, (1, 0, 2)),
        mig_count,
        jnp.transpose(segments, (1, 0, 2)).reshape(12 * blocks, width),
        remesh_matrix,
    )
    return jnp.transpose(result.reshape(12, blocks, width), (1, 0, 2))


def solution(mesh):
    return jax.shard_map(
        on_device,
        mesh=mesh,
        in_specs=(
            P(("gx", "gy", "gz"), None, None),
            P(),
            P(("gx", "gy", "gz"), None, None),
            P(("gx", "gy", "gz"), None, None),
            P(("gx", "gy", "gz")),
            P(),
            P(("gx", "gy", "gz"), None, None),
            P(("gx", "gy", "gz"), None),
        ),
        out_specs=P(("gx", "gy", "gz"), None, None),
        check_vma=False,
    )
```

```python
import functools

import jax
import jax.numpy as jnp
from jax import lax
from jax.experimental import pallas as pl
from jax.experimental.pallas import tpu as pltpu
from jax.sharding import PartitionSpec as P

STEPS = 3
MESH = pl.DeviceIdType.MESH

core_square = 0.1
time_step = 0.5
stress_coef = 0.25

GROUP = 32


TARGET, SOURCE, TERM, KEEP, LAST, RANK = 0, 4, 8, 12, 16, 17


def kernel(
    sizes,
    cut_order,
    pairs,
    used,
    ghost_list,
    lists,
    amounts,
    segments,
    remesh,
    result,
    geo,
    inv,
    matrix,
    draft,
    table,
    own_pos,
    own_b,
    near,
    far,
    terms,
    weights_a,
    weights_b,
    sums,
    field,
    remap,
    counts,
    count_out,
    count_in,
    gpos_out,
    gpos_in,
    gb_out,
    gb_in,
    inv_out,
    inv_in,
    pos_out,
    pos_in,
    vel_out,
    vel_in,
    inv_got,
    pos_got,
    vel_got,
    load_sems,
    count_local,
    count_send,
    count_recv,
    gpos_send,
    gpos_recv,
    gb_send,
    gb_recv,
    inv_send,
    inv_recv,
    pos_send,
    pos_recv,
    vel_send,
    vel_recv,
):
    blocks, tiles, ghosts, capacity = sizes
    width = segments.shape[1]
    held = blocks + capacity
    here = tuple(lax.axis_index(name) for name in ("gx", "gy", "gz"))

    def shifted(axis, by):
        count = lax.axis_size(("gx", "gy", "gz")[axis])
        place = list(here)
        place[axis] = lax.rem(here[axis] + (by % count), count)
        return tuple(place)

    neighbours = []
    for axis in range(3):
        neighbours += [shifted(axis, 1), shifted(axis, -1)]
    partners = [
        shifted(axis, lax.axis_size(name) // 2) for axis, name in enumerate(("gx", "gy", "gz"))
    ]

    def partner_of(s):
        place = []
        for axis, name in enumerate(("gx", "gy", "gz")):
            apart = s - cut_order.index(axis)
            here_cut = 1 - (apart * apart + 3) // 4
            count = lax.axis_size(name)
            place.append(lax.rem(here[axis] + here_cut * (count // 2), count))
        return tuple(place)

    barrier = pltpu.get_barrier_semaphore()
    for device in neighbours + partners:
        pl.semaphore_signal(barrier, inc=1, device_id=device, device_id_type=MESH)

    row = lax.broadcasted_iota(jnp.int32, (8, width), 0)
    upper = row < 4
    edge = (row == 3) | (row == 7)
    blank = jnp.zeros((8, width), jnp.float32)
    half_core = 0.5 * core_square

    def rows(ref, i, stride=blocks, count=8):
        return ref[pl.ds(i, count, stride=stride), :]

    def remote(source, landing, send, recv, device):
        return pltpu.make_async_remote_copy(
            src_ref=source,
            dst_ref=landing,
            send_sem=send,
            recv_sem=recv,
            device_id=device,
            device_id_type=MESH,
        )

    loads = (
        (segments.at[pl.ds(0, 3 * blocks)], geo.at[pl.ds(0, 3 * blocks)]),
        (segments.at[pl.ds(3 * blocks, 3 * blocks)], inv.at[pl.ds(0, 3 * blocks)]),
        (segments.at[pl.ds(6 * blocks, 3 * blocks)], geo.at[pl.ds(4 * blocks, 3 * blocks)]),
        (segments.at[pl.ds(9 * blocks, 3 * blocks)], inv.at[pl.ds(4 * blocks, 3 * blocks)]),
        (remesh, matrix),
    )
    loads = [
        pltpu.make_async_copy(source, landing, load_sems.at[k])
        for k, (source, landing) in enumerate(loads)
    ]
    for load in loads:
        load.start()
    for ref in (geo, inv):
        for k in (3, 7):
            ref[k * blocks : (k + 1) * blocks, :] = jnp.zeros((blocks, width), jnp.float32)
    terms[held + ghosts] = blank
    sums[tiles] = blank
    weights_b[...] = jnp.zeros_like(weights_b)
    for ref in (inv_got, pos_got, vel_got):
        ref[...] = jnp.zeros_like(ref)

    def plain(i, carry):
        remap[i] = i
        return carry

    lax.fori_loop(0, held + ghosts + 1, plain, 0, unroll=37)
    for s in range(STEPS):
        count_out[s : s + 1, :] = jnp.full((1, width), amounts[0, s], jnp.int32)

    def joined(first, second):
        return jnp.where(upper, first, pltpu.roll(second, 4, 0))

    def products(pair):
        once, twice = pair * pltpu.roll(pair, 7, 0), pair * pltpu.roll(pair, 6, 0)
        square = pair * pair
        first = jnp.where(row == 3, pltpu.roll(twice, 3, 0), pltpu.roll(once, 4, 0))
        second = jnp.where(row == 3, pltpu.roll(twice, 7, 0), once)
        return (
            jnp.where(row < 3, square, first),
            jnp.where(row < 3, pltpu.roll(square, 4, 0), second),
        )

    def features(pair, i, target):
        high = pair.astype(jnp.bfloat16).astype(jnp.float32)
        rest = pair - high
        middle = rest.astype(jnp.bfloat16).astype(jnp.float32)
        parts = (high, middle, rest - middle)
        turned = tuple(pltpu.roll(part, 4, 0) for part in parts)
        factor = jnp.where(edge, 1.0, -2.0)
        for v, (up, down) in enumerate(((parts, turned), (turned, parts))):
            mixed = jnp.where(upper, up[0], down[1])
            small = jnp.where(upper, up[2], down[1])
            stack = [
                jnp.where(edge, 1.0, jnp.where(upper, up[0], down[0])),
                jnp.where(row == 3, 1.0, mixed),
                jnp.where(row == 7, down[0], small),
                small,
            ]
            far[i + v] = jnp.concatenate(stack, axis=0).astype(jnp.bfloat16).T
            if target:
                stack = [
                    factor * mixed,
                    jnp.where(row == 7, 1.0, factor * jnp.where(upper, up[2], down[0])),
                    jnp.where(edge, 1.0, factor * mixed),
                    jnp.where(edge, 0.0, factor * jnp.where(upper, up[1], down[2])),
                ]
                near[i + v] = jnp.concatenate(stack, axis=0).astype(jnp.bfloat16)

    def prepare_own(h, c):
        i = 2 * h
        features(joined(own_pos[i], own_pos[i + 1]), i, True)
        terms[i], terms[i + 1] = products(joined(own_b[i], own_b[i + 1]))
        return c

    def ghost_copy(kind, s, face):
        source, landing, send, recv = kind
        axis, low = face // 2, face % 2
        octants = source.at[s]
        bit = 1 - low
        part = (octants.at[bit], octants.at[:, bit], octants.at[:, :, bit])[axis]
        return remote(
            part, landing.at[s, face], send.at[s, face], recv.at[s, face], neighbours[face]
        )

    ghost_pos = (gpos_out, gpos_in, gpos_send, gpos_recv)
    ghost_b = (gb_out, gb_in, gb_send, gb_recv)

    def ghost_gather(kind, block_of, s):
        for o in range(8):
            for h in range(2):
                first = block_of(remap[ghost_list[2 * h, o]])
                second = block_of(remap[ghost_list[2 * h + 1, o]])
                kind[0][s, o // 4, (o // 2) % 2, o % 2, h] = joined(first, second)
        for face in range(6):
            ghost_copy(kind, s, face).start()

    def note(line, values):
        draft[pl.ds(line * width, width)] = values[0]

    def order_pairs():
        number = lax.broadcasted_iota(jnp.int32, (1, tiles), 1)
        lane = lax.broadcasted_iota(jnp.int32, (1, width), 1)
        key = pairs[0:1, :] * tiles + number
        dead = jnp.where(number >= used[0], 1, 0)
        packed = (pairs[0:1, :] * 1024 + pairs[1:2, :]) * 2 + dead
        columns = jnp.concatenate([key, packed, jnp.zeros((6, tiles), jnp.int32)], axis=0).T
        ordered = jnp.zeros((1, tiles), jnp.int32)
        upto, before = jnp.zeros((1, width), jnp.int32), jnp.zeros((1, width), jnp.int32)
        for c in range(0, tiles, width):
            column = columns[c : c + width, 0:1]
            place = jnp.sum(jnp.where(key < column, 1, 0), axis=1, keepdims=True)
            content = columns[c : c + width, 1:2]
            ordered += jnp.sum(jnp.where(place == number, content, 0), axis=0, keepdims=True)
            upto += jnp.sum(
                jnp.where(column < (lane + 1) * tiles, 1, 0), axis=0, keepdims=True
            )
            before += jnp.sum(jnp.where(column < lane * tiles, 1, 0), axis=0, keepdims=True)
        source = lax.shift_right_logical(ordered, 1) & 1023
        source = jnp.where(source < blocks, source, source + capacity)
        target = lax.shift_right_logical(ordered, 11)
        prior = pltpu.roll(jnp.broadcast_to(target, (8, tiles)), 1, 1)[0:1]
        term = jnp.where((ordered & 1) == 1, held + ghosts, source)
        keep = jnp.where((target == prior) & (number > 0), 1, 0)
        for c in range(tiles // width):
            for part, values in ((TARGET, target), (SOURCE, source), (TERM, term), (KEEP, keep)):
                note(part + c, values[:, c * width : (c + 1) * width])
        note(LAST, jnp.where(upto > before, upto - 1, tiles))
        for s in range(STEPS):
            rank = jnp.full((1, width), capacity, jnp.int32)
            for r in range(capacity):
                rank = jnp.where(lane == lists[s, 0, r], r, rank)
            note(RANK + s, rank)

    def partner_copy(kind, s):
        source, landing, send, recv, parts = kind
        span = pl.ds(0, parts * capacity)
        return remote(
            source.at[s, span], landing.at[s, span], send.at[s], recv.at[s], partner_of(s)
        )

    moved_inv = (inv_out, inv_in, inv_send, inv_recv, 6)
    moved_pos = (pos_out, pos_in, pos_send, pos_recv, 3)
    moved_vel = (vel_out, vel_in, vel_send, vel_recv, 3)

    def count_copy(s):
        return remote(count_out, count_in.at[s], count_send.at[s], count_recv.at[s], partner_of(s))

    def collect_arrivals(kind, got, s):
        landing, parts = kind[1], kind[4]
        for k in range(parts * capacity // 8):
            span = pl.ds(8 * k, 8)
            got[span] = landing[s, span]

    def limit_of(s):
        return jnp.minimum(amounts[0, s], counts[s, s, 0])

    def entry(part, spot, u):
        return table[spot + (part * width + u)]

    def weigh(spot, u, out):
        product = jnp.dot(
            far[remap[entry(SOURCE, spot, u)]],
            near[remap[entry(TARGET, spot, u)]],
            preferred_element_type=jnp.float32,
        )
        out[...] = (1.0 / jnp.maximum(product, core_square)).astype(jnp.bfloat16)

    def add_pair(t, spot, weights, u, run):
        first = terms[remap[entry(TERM, spot, u)]]
        second = terms[remap[entry(TERM, spot, u + 1)]]
        left = jnp.concatenate([first, blank], axis=0)
        right = jnp.concatenate([blank, second], axis=0)
        both = jnp.dot(
            jnp.concatenate([left, right], axis=1).astype(jnp.bfloat16),
            jnp.concatenate([weights[u], weights[u + 1]], axis=0),
            preferred_element_type=jnp.float32,
        )
        for v in range(2):
            run = jnp.where(entry(KEEP, spot, u + v) != 0, run, 0.0) + both[8 * v : 8 * v + 8]
            sums[t + u + v] = run
        return run

    def spot_of(g):
        return g * GROUP

    groups = tiles // GROUP

    def half(g, run, fill, ready):
        past = lax.rem(g + groups - 1, groups)
        spot, before = spot_of(g), spot_of(past)
        for u in range(0, GROUP, 2):
            for v in range(2):
                weigh(spot, u + v, fill.at[u + v])
            run = add_pair(past * GROUP, before, ready, u, run)
        return run

    def two_groups(h, run):
        run = half(2 * h, run, weights_a, weights_b)
        return half(2 * h + 1, run, weights_b, weights_a)

    def collect(i, c):
        field[pl.ds(i, 8, stride=blocks), :] = sums[table[LAST * width + i]]
        return c

    def comp(ref, k):
        return ref[k * blocks : (k + 1) * blocks, :]

    def settle(s, pieces):
        limit = limit_of(s)

        def body(i, c):
            r = table[(RANK + s) * width + i]
            spot = jnp.minimum(r, capacity - 1)
            for ref, base, got, first, parts, *target in pieces:
                span = pl.ds(base * blocks + i, parts, stride=blocks)
                arrived = rows(got, first * capacity + spot, capacity, parts)
                fresh = jnp.where(r < limit, arrived, ref[span, :])
                if target:
                    out, at = target
                    out[pl.ds(at * blocks + i, parts, stride=blocks), :] = fresh
                else:
                    ref[span, :] = fresh
            return c

        lax.fori_loop(0, blocks, body, 0, unroll=8)

    placed = ((geo, 0, pos_got, 0, 3), (inv, 0, inv_got, 0, 3), (inv, 4, inv_got, 3, 3))

    def norm_of(ref, count):
        x, y, z = (ref[k * count : (k + 1) * count, :] for k in range(3))
        return x * x + y * y + z * z + half_core

    def advance():
        scale = stress_coef / width
        sxx, syy, szz = (comp(field, k) * scale for k in (0, 1, 2))
        sxy, syz, sxz = (comp(field, k) * scale for k in (4, 5, 3))
        b = [comp(inv, k) for k in (0, 1, 2)]
        force = (
            sxx * b[0] + sxy * b[1] + sxz * b[2],
            sxy * b[0] + syy * b[1] + syz * b[2],
            sxz * b[0] + syz * b[1] + szz * b[2],
        )
        for k in range(3):
            velocity = comp(inv, 4 + k) * force[k]
            previous = comp(geo, 4 + k)
            geo[k * blocks : (k + 1) * blocks, :] = comp(geo, k) + time_step * (
                1.5 * velocity - 0.5 * previous
            )
            geo[(4 + k) * blocks : (5 + k) * blocks, :] = velocity
        geo[0 : 3 * blocks, :] = jnp.dot(
            geo[0 : 3 * blocks, :],
            matrix[...],
            precision=lax.Precision.HIGHEST,
            preferred_element_type=jnp.float32,
        )
        geo[3 * blocks : 4 * blocks, :] = norm_of(geo, blocks)

    def gather_out(s, outs):
        def body(r, c):
            slot = lists[s, 0, r]
            for ref, base, out, first, parts in outs:
                block = ref[pl.ds(base * blocks + slot, parts, stride=blocks), :]
                out[s, pl.ds(first * capacity + r, parts, stride=capacity), :] = block
            return c

        lax.fori_loop(0, capacity, body, 0, unroll=8)

    order_pairs()
    ordering = pltpu.make_async_copy(draft, table, load_sems.at[5])
    ordering.start()
    for load in loads[:4]:
        load.wait()
    geo[3 * blocks : 4 * blocks, :] = norm_of(geo, blocks)
    pl.semaphore_wait(barrier, 9)
    ghost_gather(ghost_pos, lambda pick: rows(geo, pick), 0)
    ghost_gather(ghost_b, lambda pick: rows(inv, pick), 0)
    for s in range(STEPS):
        count_copy(s).start()
    for load in loads[4:]:
        load.wait()

    def refresh(i, c):
        own_pos[i] = rows(geo, i)
        own_b[i] = rows(inv, i)
        return c

    lax.fori_loop(0, blocks, refresh, 0, unroll=8)
    lax.fori_loop(0, blocks // 2, prepare_own, 0, unroll=8)
    for s in range(STEPS):
        count_copy(s).wait_recv()
    local = pltpu.make_async_copy(count_in, counts, count_local)
    local.start()
    local.wait()
    ordering.wait()

    def step(s, carry):
        @pl.when(s > 0)
        def _():
            lax.fori_loop(blocks // 2, held // 2, prepare_own, 0, unroll=6)
            settle(s - 1, placed)

        gather_out(s, ((inv, 0, inv_out, 0, 3), (inv, 4, inv_out, 3, 3)))
        for face in range(6):
            ghost_copy(ghost_b, s, face).wait_recv()

        def ghost_terms(face, c):
            for k in range(8):
                spot = held + face * 16 + 2 * k
                pair = gb_in[s, face, k // 4, (k // 2) % 2, k % 2]
                terms[spot], terms[spot + 1] = products(pair)
            return c

        lax.fori_loop(0, 6, ghost_terms, 0, unroll=2)
        for face in range(6):
            ghost_copy(ghost_pos, s, face).wait_recv()

        def ghost_features(face, c):
            for k in range(8):
                spot = held + face * 16 + 2 * k
                features(gpos_in[s, face, k // 4, (k // 2) % 2, k % 2], spot, False)
            return c

        lax.fori_loop(0, 6, ghost_features, 0, unroll=2)
        partner_copy(moved_inv, s).start()

        @pl.when(s > 0)
        def _():
            partner_copy(moved_vel, s - 1).start()

        run = lax.fori_loop(0, groups // 2, two_groups, blank)
        for u in range(0, GROUP, 2):
            run = add_pair((groups - 1) * GROUP, spot_of(jnp.int32(groups - 1)), weights_b, u, run)
        lax.fori_loop(0, blocks, collect, 0, unroll=8)

        @pl.when(s > 0)
        def _():
            partner_copy(moved_vel, s - 1).wait_recv()
            collect_arrivals(moved_vel, vel_got, s - 1)
            settle(s - 1, ((geo, 4, vel_got, 0, 3),))

        advance()
        gather_out(s, ((geo, 0, pos_out, 0, 3),))
        partner_copy(moved_pos, s).start()
        gather_out(s, ((geo, 4, vel_out, 0, 3),))

        @pl.when(s == STEPS - 1)
        def _():
            partner_copy(moved_vel, s).start()

        partner_copy(moved_inv, s).wait_recv()
        collect_arrivals(moved_inv, inv_got, s)

        @pl.when(s < STEPS - 1)
        def _():
            limit = limit_of(s)

            def route(i, c):
                r = table[(RANK + s) * width + i]
                remap[i] = jnp.where(r < limit, blocks + r, i)
                return c

            lax.fori_loop(0, blocks, route, 0, unroll=8)

            def arrive_b(r, c):
                own_b[blocks + r] = rows(inv_got, r, capacity)
                return c

            lax.fori_loop(0, capacity, arrive_b, 0, unroll=8)
            lax.fori_loop(0, blocks, refresh, 0, unroll=8)
            ghost_gather(ghost_b, lambda pick: own_b[pick], s + 1)
            lax.fori_loop(0, blocks // 2, prepare_own, 0, unroll=8)

        @pl.when(s == STEPS - 1)
        def _():
            final = ((inv, 0, inv_got, 0, 3, result, 3), (inv, 4, inv_got, 3, 3, result, 9))
            settle(s, final)

        partner_copy(moved_pos, s).wait_recv()
        collect_arrivals(moved_pos, pos_got, s)

        @pl.when(s < STEPS - 1)
        def _():
            pos_got[3 * capacity : 4 * capacity, :] = norm_of(pos_got, capacity)

            def arrive(r, c):
                own_pos[blocks + r] = rows(pos_got, r, capacity)
                return c

            lax.fori_loop(0, capacity, arrive, 0, unroll=8)
            ghost_gather(ghost_pos, lambda pick: own_pos[pick], s + 1)

        for face in range(6):
            ghost_copy(ghost_b, s, face).wait_send()
            ghost_copy(ghost_pos, s, face).wait_send()
        partner_copy(moved_inv, s).wait_send()
        partner_copy(moved_pos, s).wait_send()
        return carry

    lax.fori_loop(0, STEPS, step, 0)
    last = STEPS - 1
    settle(last, ((geo, 0, pos_got, 0, 3, result, 0),))
    partner_copy(moved_vel, last).wait_recv()
    collect_arrivals(moved_vel, vel_got, last)
    settle(last, ((geo, 4, vel_got, 0, 3, result, 6),))
    for s in range(STEPS):
        count_copy(s).wait_send()
        partner_copy(moved_vel, s).wait_send()


def on_device(
    segments, remesh_matrix, ghost_list, pair_list, tile_count, cut_axis, mig_list, mig_count
):
    blocks, _, width = segments.shape
    tiles = pair_list.shape[1]
    per_cell = ghost_list.shape[2]
    ghosts = 24 * per_cell
    capacity = mig_list.shape[2]
    vmem, smem = (pl.BlockSpec(memory_space=m) for m in (pltpu.VMEM, pltpu.SMEM))
    f32, bf16 = jnp.float32, jnp.bfloat16
    held = blocks + capacity
    scratch = [
        pltpu.VMEM((8 * blocks, width), f32),
        pltpu.VMEM((8 * blocks, width), f32),
        pltpu.VMEM((width, width), f32),
        pltpu.VMEM((24 * width,), jnp.int32),
        pltpu.SMEM((24 * width,), jnp.int32),
        pltpu.VMEM((held, 8, width), f32),
        pltpu.VMEM((held, 8, width), f32),
        pltpu.VMEM((held, 32, width), bf16),
        pltpu.VMEM((held + ghosts, width, 32), bf16),
        pltpu.VMEM((held + ghosts + 1, 8, width), f32),
        pltpu.VMEM((GROUP, width, width), bf16),
        pltpu.VMEM((GROUP, width, width), bf16),
        pltpu.VMEM((tiles + 1, 8, width), f32),
        pltpu.VMEM((8 * blocks, width), f32),
        pltpu.SMEM((held + ghosts + 1,), jnp.int32),
        pltpu.SMEM((STEPS, 8, width), jnp.int32),
        pltpu.VMEM((8, width), jnp.int32),
        pltpu.VMEM((STEPS, 8, width), jnp.int32),
        pltpu.VMEM((STEPS, 2, 2, 2, per_cell // 2, 8, width), f32),
        pltpu.VMEM((STEPS, 6, 2, 2, per_cell // 2, 8, width), f32),
        pltpu.VMEM((STEPS, 2, 2, 2, per_cell // 2, 8, width), f32),
        pltpu.VMEM((STEPS, 6, 2, 2, per_cell // 2, 8, width), f32),
        pltpu.VMEM((STEPS, 8 * capacity, width), f32),
        pltpu.VMEM((STEPS, 8 * capacity, width), f32),
        pltpu.VMEM((STEPS, 8 * capacity, width), f32),
        pltpu.VMEM((STEPS, 8 * capacity, width), f32),
        pltpu.VMEM((STEPS, 8 * capacity, width), f32),
        pltpu.VMEM((STEPS, 8 * capacity, width), f32),
        pltpu.VMEM((8 * capacity, width), f32),
        pltpu.VMEM((8 * capacity, width), f32),
        pltpu.VMEM((8 * capacity, width), f32),
        pltpu.SemaphoreType.DMA((6,)),
        pltpu.SemaphoreType.DMA,
        pltpu.SemaphoreType.DMA((STEPS,)),
        pltpu.SemaphoreType.DMA((STEPS,)),
        pltpu.SemaphoreType.DMA((STEPS, 6)),
        pltpu.SemaphoreType.DMA((STEPS, 6)),
        pltpu.SemaphoreType.DMA((STEPS, 6)),
        pltpu.SemaphoreType.DMA((STEPS, 6)),
        pltpu.SemaphoreType.DMA((STEPS,)),
        pltpu.SemaphoreType.DMA((STEPS,)),
        pltpu.SemaphoreType.DMA((STEPS,)),
        pltpu.SemaphoreType.DMA((STEPS,)),
        pltpu.SemaphoreType.DMA((STEPS,)),
        pltpu.SemaphoreType.DMA((STEPS,)),
    ]
    orders = [(0, 1, 2), (0, 2, 1), (1, 0, 2), (1, 2, 0), (2, 0, 1), (2, 1, 0)]

    def with_order(number):
        return pl.pallas_call(
            functools.partial(kernel, (blocks, tiles, ghosts, capacity), orders[number]),
            out_shape=jax.ShapeDtypeStruct((12 * blocks, width), f32),
            in_specs=[vmem] + [smem] * 4 + [pl.BlockSpec(memory_space=pltpu.HBM)] * 2,
            out_specs=vmem,
            scratch_shapes=scratch,
            compiler_params=pltpu.CompilerParams(
                collective_id=number, has_side_effects=True, vmem_limit_bytes=63 * 1024 * 1024
            ),
        )

    code = jnp.sum(cut_axis * jnp.maximum(3 - 2 * jnp.arange(STEPS, dtype=jnp.int32), 0))
    number = code - 1 - lax.shift_right_logical(code, 2)
    result = lax.switch(
        number,
        [with_order(k) for k in range(6)],
        pair_list[0].T,
        tile_count,
        ghost_list[0].T,
        jnp.transpose(mig_list, (1, 0, 2)),
        mig_count,
        jnp.transpose(segments, (1, 0, 2)).reshape(12 * blocks, width),
        remesh_matrix,
    )
    return jnp.transpose(result.reshape(12, blocks, width), (1, 0, 2))


def solution(mesh):
    return jax.shard_map(
        on_device,
        mesh=mesh,
        in_specs=(
            P(("gx", "gy", "gz"), None, None),
            P(),
            P(("gx", "gy", "gz"), None, None),
            P(("gx", "gy", "gz"), None, None),
            P(("gx", "gy", "gz")),
            P(),
            P(("gx", "gy", "gz"), None, None),
            P(("gx", "gy", "gz"), None),
        ),
        out_specs=P(("gx", "gy", "gz"), None, None),
        check_vma=False,
    )
```
